256 devices in a mesh: row: 16 (over x, y), col: 8 (over z_lo, core), layer: 2 (over z_hi).
Axes of the slice: x: 4, y: 4, z: 8 (z_hi: 2, z_lo: 4; z = z_hi * 4 + z_lo), core: 2. Of those that a mesh axis runs over, the one named last changes fastest.
Arguments:
- tasks: bfloat16 [16384, 4096], P(('row', 'col')), may hold values from -0.1875 to 0.1875
- task_owner: int32 [16384, 1], P(('row', 'col')), may hold values from 0 to 127; in each aligned block of 128 rows (0 to 127, 128 to 255, ...) at most 2 rows name the same one
- task_slot: int32 [16384], P(('row', 'col')), may hold values from 0 to 127
- p_pattern: int32 [128, 128], P('row', 'col'), may hold values from 0 to 1, as said below
- c_pattern: int32 [128, 128], P('row', 'col'), may hold values from 0 to 1, as said below
- occupations: float32 [8192], P('row'), may hold values from 0.1 to 0.9
Outputs:
- purified: float32 [8192, 8192], P(('row', 'layer'), 'col')
The draws below stay inside these ranges and needn't reach their ends.
Inputs may be any that keep to these rules, and one draw needn't show every extreme that they name: `task_owner`: the 128 tasks of one index of row and col name each owner at most 2 times. `task_slot`: a block of the owner's 8 x 16 blocks, row-major. `p_pattern`: 0 or 1; every diagonal block is 1. `c_pattern`: 0 or 1; every diagonal block is 1.
All inputs are finite; a program needn't handle non-finite values.
Results may differ from the reference program's by a relative error of at most 0.025.
Values may be sent and summed in bfloat16 or wider, within the bound.
A program may use at most 64 MiB of HBM per device.

```python
import math
import jax
import jax.numpy as jnp
import numpy as np
from jax import lax

BLK = 64
RB_DEV = 8
TASK_DEV = 128
NB = 128
ORDER = 8192
CB_DEV = 16
CAP = 2
TASKS = 16384
N_ROW = 16
N_COL = 8


def banded(key, near, far):
    index = jnp.arange(NB, dtype=jnp.int32)
    spread = jnp.abs(index[:, None] - index[None, :])
    spread = jnp.minimum(spread, NB - spread)
    chance = near - (near - far) * 2 * spread // max(NB, 1)
    roll = jax.random.randint(key, (NB, NB), 0, 1000, dtype=jnp.int32)
    return jnp.where((roll < chance) | (spread == 0), 1, 0).astype(jnp.int32)


def draw_p_pattern(key, part):
    return banded(jax.random.fold_in(key, 11), 900, 150)


def draw_c_pattern(key, part):
    return banded(jax.random.fold_in(key, 23), 950, 300)


def place_ends(entries, own_key, smallest, largest):
    place = [jax.random.randint(jax.random.fold_in(own_key, axis), (), 0, length) for axis, length in enumerate(entries.shape)]
    main_axis = entries.shape.index(max(entries.shape))
    next_to = place[:main_axis] + [(place[main_axis] + 1) % entries.shape[main_axis]] + place[main_axis + 1:]
    return entries.at[tuple(place)].set(smallest).at[tuple(next_to)].set(largest)


def block_levels(rng, dims, split, low, top_value):
    gain, own = 1.0, jax.random.fold_in(rng, 6)
    for position, parts in split:
        steps = jnp.exp(jax.random.uniform(jax.random.fold_in(own, position), (parts,), jnp.float32, low / len(split), top_value / len(split)))
        gain = gain * jnp.repeat(steps, dims[position] // parts).reshape([-1 if axis == position else 1 for axis in range(len(dims))])
    return gain


def assign_block(rng, own, number, rows, amount, top, reach, lean):
    sequence = jax.random.permutation(rng, amount)
    heavy_load, ordinary = shares(amount, rows * top, reach, lean, True), shares(amount, rows * top, reach, lean, False)
    places = jnp.arange(amount)

    def named(tallies, rotation):
        used = int((tallies > 0).sum())
        fixed = max(1, used // 4)
        shifted = fixed + (places - fixed + rotation * (used - fixed)) % max(1, amount - fixed)
        return jnp.zeros((amount,), jnp.int32).at[sequence[jnp.where(places < fixed, places, shifted)]].set(jnp.asarray(tallies, jnp.int32))

    tallies = jnp.where(number % 4 == 0, named(heavy_load, number // 4), named(ordinary, number - number // 4 - 1))
    mixed = jax.random.permutation(jax.random.fold_in(own, 3), amount)
    donor, receiver = mixed[0:amount // 2 * 2:2], mixed[1:amount // 2 * 2:2]
    margin = jnp.minimum(tallies[donor] - 1, reach - tallies[receiver]) // 2
    margin = jnp.where((donor == sequence[0]) | (receiver == sequence[0]) | (tallies[receiver] == 0), 0, jnp.maximum(margin, 0))
    shifted = jax.random.randint(jax.random.fold_in(own, 4), (amount // 2,), 0, 1 << 20) % (margin + 1)
    tallies = tallies.at[donor].add(-shifted).at[receiver].add(shifted)
    labels = jnp.searchsorted(jnp.cumsum(tallies), jnp.arange(rows * top), side="right").astype(jnp.int32)
    listing = labels.reshape(top, rows).T
    listing = listing[jax.random.permutation(jax.random.fold_in(own, 1), rows)]
    rotation = jax.random.randint(jax.random.fold_in(own, 2), (rows, 1), 0, top)
    return jnp.take_along_axis(listing, (jnp.arange(top)[None, :] + rotation) % top, axis=1)


def shares(count, total, bound, skew, full):
    portions = [(1 << 20) // math.isqrt(grade ** skew) + 1 for grade in range(1, count + 1)]
    largest = bound if full else min(bound, max(-(-total // count), total * portions[0] // sum(portions)))
    least = 1 if total - largest >= count - 1 else 0
    given, surplus = [largest] + [least] * (count - 1), total - largest - least * (count - 1)
    while surplus > 0:
        movable = [i for i in range(1, count) if given[i] < largest] or [i for i in range(1, count) if given[i] < bound]
        pool, remaining = sum([portions[i] for i in movable]), surplus
        for i in movable:
            more = min(bound - given[i], max(1, remaining * portions[i] // pool), surplus)
            given[i] = given[i] + more
            surplus = surplus - more
    return np.array(given)


def centred(key, extent, scale, bound, pieces=(), held_as=jnp.bfloat16):
    loudness = block_levels(key, extent, pieces, -0.22, 0.18) if pieces else 1.0
    array = jax.random.normal(key, extent, jnp.float32) * scale * loudness
    return jnp.minimum(jnp.maximum(array, -bound), bound).astype(held_as)


def setup_inputs(seed: int = 0) -> dict:
    key_list = jax.random.split(jax.random.key(seed), 7)
    tasks = centred(key_list[0], (TASKS, BLK * BLK), (0.8 * (NB / (32 * TASKS)) ** 0.5), 0.1875, ((0, 128),))
    task_owner_keys = jax.random.split(jax.random.fold_in(key_list[1], 1), TASKS // TASK_DEV)
    task_owner_turns = jax.random.permutation(jax.random.fold_in(key_list[1], 3), TASKS // TASK_DEV)
    task_owner = jax.vmap(lambda own, number: assign_block(jax.random.fold_in(key_list[1], 2), own, number, TASK_DEV, N_ROW * N_COL, 1, CAP, 2))(task_owner_keys, task_owner_turns).reshape((TASKS, 1))
    task_slot = place_ends(jax.random.randint(key_list[2], (TASKS,), 0, RB_DEV * CB_DEV), jax.random.fold_in(key_list[2], 1), 0, (RB_DEV * CB_DEV) - 1).astype(jnp.int32)
    p_pattern = draw_p_pattern(jax.random.fold_in(key_list[6], 71), 0)
    c_pattern = draw_c_pattern(jax.random.fold_in(key_list[6], 71), 0)
    occupations = jnp.clip(0.1 + 0.79999997 * jax.random.uniform(key_list[5], (ORDER,), jnp.float32) ** block_levels(key_list[5], (ORDER,), ((0, 16),), -0.2, 0.2), 0.1, 0.9)
    return {"tasks": tasks, "task_owner": task_owner, "task_slot": task_slot, "p_pattern": p_pattern, "c_pattern": c_pattern, "occupations": occupations}


def expand(pattern):
    return jnp.repeat(jnp.repeat(pattern.astype(jnp.float32), BLK, axis=0), BLK, axis=1)


def reference(tasks, task_owner, task_slot, p_pattern, c_pattern, occupations):
    owner = task_owner[:, 0]
    grid_cols = NB // CB_DEV
    block_row = (owner // grid_cols) * RB_DEV + task_slot // CB_DEV
    block_col = (owner % grid_cols) * CB_DEV + task_slot % CB_DEV
    target = (block_row * NB + block_col).astype(jnp.int32)
    blocks = jnp.zeros((NB * NB, BLK * BLK), jnp.float32).at[target].add(tasks.astype(jnp.float32))
    assembled = blocks.reshape(NB, NB, BLK, BLK).transpose(0, 2, 1, 3).reshape(ORDER, ORDER)
    density = (expand(p_pattern) * assembled + jnp.diag(occupations)).astype(jnp.bfloat16)
    wide = density.astype(jnp.float32)
    square = jnp.dot(wide, wide, precision=lax.Precision.HIGHEST)
    square_low = lax.optimization_barrier(square.astype(jnp.bfloat16)).astype(jnp.float32)
    cube = jnp.dot(wide, square_low, precision=lax.Precision.HIGHEST)
    return expand(c_pattern) * (3.0 * square - 2.0 * cube)
```

```python
import functools

import jax
import jax.numpy as jnp
from jax import lax
from jax.experimental import pallas as pl
from jax.experimental.pallas import tpu as pltpu
from jax.sharding import PartitionSpec as P

BLK = 64
HALF = 32
MESH = pl.DeviceIdType.MESH
BF16 = jnp.bfloat16
F32 = jnp.float32


def iota(shape, axis):
    return lax.broadcasted_iota(jnp.int32, shape, axis)


def dot(a, b):
    return jnp.dot(a, b, preferred_element_type=F32)


def pack_kernel(task_ref, owner_col_ref, owner_row_ref, slot_ref, out_ref):
    count = task_ref.shape[0]
    half = lax.axis_index("layer")
    earlier = iota((count, count), 0) < iota((count, count), 1)
    same = (owner_col_ref[...] == owner_row_ref[...]) & earlier
    placed = jnp.sum(same.astype(jnp.int32), axis=0, keepdims=True)
    target = owner_row_ref[...] * 2 + placed
    put = (iota((2 * count, count), 0) == target).astype(BF16)
    lane = iota((256, 128), 0)
    want = iota((256, 128), 1)
    source = (want // HALF) * BLK + half * HALF + want % HALF
    pick = (lane == source).astype(BF16)
    for group in range(task_ref.shape[1] // 256):
        piece = dot(task_ref[:, group * 256 : (group + 1) * 256], pick).astype(BF16)
        out_ref[:, group * 128 : (group + 1) * 128] = dot(put, piece).astype(BF16)
    slot = slot_ref[...]
    order = (slot % 16) * 8 + slot // 16
    marks = jnp.broadcast_to(order + 1, (count, 128)).astype(BF16)
    out_ref[:, 2048:2176] = (dot(put, marks) - 1.0).astype(BF16)


def assemble_kernel(got_ref, pattern_ref, occ_ref, out_ref, rows):
    row_id = lax.axis_index("row") * 512
    col_id = lax.axis_index("col") * 1024 + lax.axis_index("layer") * HALF
    entries = got_ref.shape[0]
    marks = (got_ref[:, 2048:2176].astype(F32) == iota((entries, 128), 1).astype(F32)).astype(BF16)
    spread = (iota((16, 512), 0) == iota((16, 512), 1) // HALF).astype(F32)
    mask = dot(pattern_ref[...].astype(F32), spread)
    column = col_id + (iota((8, 512), 1) // HALF) * BLK + iota((8, 512), 1) % HALF
    first = row_id + iota((8, 512), 0) * BLK
    quarter = iota((8, 128), 1) // HALF
    for quad in range(16):
        summed = lax.dot_general(
            marks,
            got_ref[:, quad * 128 : (quad + 1) * 128],
            (((0,), (0,)), ((), ())),
            preferred_element_type=F32,
        )
        for e in range(4):
            tiles = []
            for t in range(4):
                tile = None
                for f in range(4):
                    block = t * 4 + f
                    value = summed[block * 8 : (block + 1) * 8, :]
                    shift = (f - e) % 4
                    if shift:
                        value = pltpu.roll(value, shift * HALF, 1)
                    tile = value if tile is None else jnp.where(quarter == f, value, tile)
                tiles.append(tile)
            i = quad * 4 + e
            line = jnp.concatenate(tiles, axis=1) * mask
            line = line + jnp.where(first + i == column, occ_ref[:, i : i + 1], 0.0)
            rows[i * 8 : (i + 1) * 8, :] = line
    want = iota((256, 256), 0)
    have = iota((256, 256), 1)
    move = (have == (want % HALF) * 8 + want // HALF).astype(BF16)
    for h in range(2):
        out_ref[h] = dot(move, rows[h * 256 : (h + 1) * 256, :].astype(BF16)).astype(BF16)


def step_kernel(
    d_ref, pattern_ref, out_ref,
    a, b, b2, acc, keep, near, far, near_in, far_in, mixed, swapped,
    local_sem, y_send, y_recv, z_send, z_recv, twin_send, twin_recv,
    x_send, x_recv, r_send, r_recv, swap_send, swap_recv,
):
    row, col, layer = lax.axis_index("row"), lax.axis_index("col"), lax.axis_index("layer")
    x, y = row // 4, row % 4
    core = col % 2
    z = layer * 4 + col // 2

    def device(xx, yy, zz, cc):
        return (xx * 4 + yy, (zz % 4) * 2 + cc, zz // 4)

    def ring(value, step, size):
        return (value + step + size) % size

    twin = device(x, y, z, 1 - core)
    up_y, down_y = device(x, ring(y, 1, 4), z, core), device(x, ring(y, -1, 4), z, core)
    up_x, down_x = device(ring(x, 1, 4), y, z, core), device(ring(x, -1, 4), y, z, core)
    up_z, down_z = device(x, y, ring(z, 1, 8), core), device(x, y, ring(z, -1, 8), core)
    across = device(x, y, ring(z, 4, 8), core)

    barrier = pltpu.get_barrier_semaphore()
    others = [device(x, ring(y, s, 4), z, c) for s in range(1, 4) for c in range(2)]
    others += [twin, up_x, down_x, up_z, down_z, across]
    for other in others:
        pl.semaphore_signal(barrier, inc=1, device_id=other, device_id_type=MESH)
    pl.semaphore_wait(barrier, len(others))

    def remote(src, dst, send, recv, to):
        return pltpu.make_async_remote_copy(
            src_ref=src, dst_ref=dst, send_sem=send, recv_sem=recv, device_id=to, device_id_type=MESH
        )

    y_copies = []
    for p in range(2):
        for c in range(2):
            to_y = 2 * core + p
            mine = jnp.logical_and(to_y == y, core == c)
            src = d_ref.at[c, :, pl.ds(p * 256, 256)]
            dst = a.at[z, c * 4 + y]
            copy = remote(src, dst, y_send.at[p * 2 + c], y_recv.at[y], device(x, to_y, z, c))
            own = pltpu.make_async_copy(src, dst, local_sem.at[0])

            @pl.when(jnp.logical_not(mine))
            def _():
                copy.start()

            @pl.when(mine)
            def _():
                own.start()

            y_copies.append((mine, copy, own))

    def x_first(source, panel, sems):
        up = remote(source, panel.at[:, x], x_send.at[sems], x_recv.at[sems], up_x)
        down = remote(source, panel.at[:, x], x_send.at[sems + 1], x_recv.at[sems + 1], down_x)
        home = pltpu.make_async_copy(source, panel.at[:, x], local_sem.at[1 + sems // 4])
        up.start()
        down.start()
        home.start()
        return up, down, home

    def x_second(panel, sems, first):
        first[0].wait_recv()
        left = ring(x, -1, 4)
        up = remote(panel.at[0, left], panel.at[0, left], x_send.at[sems + 2], x_recv.at[sems + 2], up_x)
        up.start()
        first[1].wait_recv()
        right = ring(x, 1, 4)
        down = remote(panel.at[1, right], panel.at[1, right], x_send.at[sems + 3], x_recv.at[sems + 3], down_x)
        down.start()
        return up, down

    x_one = x_first(d_ref, b, 0)

    for source_y in range(4):
        mine = jnp.logical_and(y == source_y, core == y // 2)
        block = a.at[z, core * 4 + source_y]

        @pl.when(jnp.logical_not(mine))
        def _():
            remote(block, block, y_send.at[0], y_recv.at[source_y], twin).wait_recv()

        @pl.when(mine)
        def _():
            pltpu.make_async_copy(block, block, local_sem.at[0]).wait()

    def part(zz, low, size):
        return a.at[zz, pl.ds(core * 4 + low, size)]

    pending = []

    def z_send_step(step):
        up_block, down_block = ring(z, 1 - step, 8), ring(z, step - 1, 8)
        size = 4 if step < 4 else 2
        ups = part(up_block, 0, size)
        downs = part(down_block, 4 - size, size)
        up = remote(ups, ups, z_send.at[step - 1], z_recv.at[step - 1], up_z)
        down = remote(downs, downs, z_send.at[step + 3], z_recv.at[step + 3], down_z)
        up.start()
        down.start()
        return up, down

    def twin_send_step(index, zz, low, size):
        ref = part(zz, low, size)
        copy = remote(ref, ref, twin_send.at[index], twin_recv.at[index], twin)
        copy.start()
        pending.append(copy)

    def twin_wait(index, zz, low, size):
        ref = a.at[zz, pl.ds((1 - core) * 4 + low, size)]
        remote(ref, ref, twin_send.at[index], twin_recv.at[index], twin).wait_recv()

    def hand_over(step):
        size = 4 if step < 4 else 2
        twin_send_step(2 * step - 1, ring(z, -step, 8), 0, size)
        twin_send_step(2 * step, ring(z, step, 8), 4 - size, size)

    def take_over(step):
        size = 4 if step < 4 else 2
        twin_wait(2 * step - 1, ring(z, -step, 8), 0, size)
        twin_wait(2 * step, ring(z, step, 8), 4 - size, size)

    def product(blocks, right, first):
        pieces = [(zz, right[zz // 4, zz % 4]) for zz in blocks]

        def body(m, carry):
            total = None
            for zz, piece in pieces:
                term = dot(a[zz, m], piece)
                total = term if total is None else total + term
            acc[m] = total if first else acc[m] + total
            return carry

        lax.fori_loop(0, 8, body, 0)

    z_one = z_send_step(1)
    twin_send_step(0, z, 0, 4)
    x_two = x_second(b, 0, x_one)
    for copy in z_one:
        copy.wait_recv()
    z_two = z_send_step(2)
    hand_over(1)
    for copy in x_two:
        copy.wait_recv()
    x_one[2].wait()
    twin_wait(0, z, 0, 4)
    product([z], b, True)
    take_over(1)
    product([ring(z, -1, 8), ring(z, 1, 8)], b, False)
    for copy in z_two:
        copy.wait_recv()
    z_three = z_send_step(3)
    hand_over(2)
    take_over(2)
    product([ring(z, -2, 8), ring(z, 2, 8)], b, False)
    for copy in z_three:
        copy.wait_recv()
    z_four = z_send_step(4)
    hand_over(3)
    take_over(3)
    product([ring(z, -3, 8), ring(z, 3, 8)], b, False)
    for copy in z_four:
        copy.wait_recv()
    hand_over(4)
    take_over(4)
    product([ring(z, 4, 8)], b, False)

    def reduce(index):
        up_t, down_t, far_t = ring(y, 1, 4), ring(y, -1, 4), ring(y, 2, 4)
        base = index * 6

        def send(k, src, dst, to):
            copy = remote(src, dst, r_send.at[base + k], r_recv.at[base + k], to)
            copy.start()
            return copy

        far[index, 0] = acc[far_t].astype(BF16)
        far_up = send(0, far.at[index, 0], far_in.at[index, 0], up_y)
        far[index, 1] = acc[4 + far_t].astype(BF16)
        far_down = send(1, far.at[index, 1], far_in.at[index, 1], down_y)
        near[index, 0, 1] = acc[4 + up_t].astype(BF16)
        up_plain = send(2, near.at[index, 0, 1], near_in.at[index, 0, 1], up_y)
        near[index, 1, 0] = acc[down_t].astype(BF16)
        down_plain = send(3, near.at[index, 1, 0], near_in.at[index, 1, 0], down_y)
        far_up.wait_recv()
        near[index, 0, 0] = (acc[up_t] + far_in[index, 0].astype(F32)).astype(BF16)
        up_sum = send(4, near.at[index, 0, 0], near_in.at[index, 0, 0], up_y)
        far_down.wait_recv()
        near[index, 1, 1] = (acc[4 + down_t] + far_in[index, 1].astype(F32)).astype(BF16)
        down_sum = send(5, near.at[index, 1, 1], near_in.at[index, 1, 1], down_y)
        copies = [far_up, far_down, up_plain, down_plain, up_sum, down_sum]
        for copy in copies[2:]:
            copy.wait_recv()
        for copy in copies:
            copy.wait_send()
        return [
            acc[half * 4 + y] + near_in[index, 0, half].astype(F32) + near_in[index, 1, half].astype(F32)
            for half in range(2)
        ]

    square = reduce(0)
    for half in range(2):
        keep[half] = square[half]
        mixed[half] = square[half].astype(BF16)
    x_three = x_first(mixed, b2, 4)
    x_three[2].wait()
    product([x, x + 4], b2, True)
    x_four = x_second(b2, 4, x_three)
    left, right = ring(x, -1, 4), ring(x, 1, 4)
    product([left, left + 4, right, right + 4], b2, False)
    for copy in x_four:
        copy.wait_recv()
    opposite = ring(x, 2, 4)
    product([opposite, opposite + 4], b2, False)
    for copy in x_three[:2]:
        copy.wait_send()
    cube = reduce(1)
    for half in range(2):
        mixed[half] = (3.0 * keep[half] - 2.0 * cube[half]).astype(BF16)

    swap = remote(
        mixed.at[:, pl.ds((1 - layer) * 128, 128)], swapped, swap_send, swap_recv, across
    )
    swap.start()
    spread = (iota((16, 1024), 0) == iota((16, 1024), 1) // BLK).astype(F32)
    mask_all = dot(pattern_ref[...].astype(F32), spread)
    mask = jnp.where(layer == 0, mask_all[0:4], mask_all[4:8])
    source = iota((256, 256), 0)
    want = iota((256, 256), 1)
    side = jnp.where(source < 128, layer, 1 - layer)
    goes = ((source % 128) // HALF) * BLK + side * HALF + source % HALF
    place = (goes == want).astype(BF16)
    swap.wait_recv()
    for half in range(2):
        own = mixed[half, pl.ds(layer * 128, 128), :]
        other = swapped[half]
        for t in range(4):
            both = jnp.concatenate([own[:, t * 128 : (t + 1) * 128], other[:, t * 128 : (t + 1) * 128]], axis=1)
            full = dot(both, place)
            for blk in range(4):
                out_ref[blk * BLK + half * HALF : blk * BLK + (half + 1) * HALF, t * 256 : (t + 1) * 256] = (
                    full[blk * HALF : (blk + 1) * HALF] * mask[blk : blk + 1, t * 256 : (t + 1) * 256]
                )
    swap.wait_send()

    for mine, copy, own in y_copies:
        @pl.when(jnp.logical_not(mine))
        def _():
            copy.wait_send()

    for copy in (*x_one[:2], *x_two, *x_four, *z_one, *z_two, *z_three, *z_four, *pending):
        copy.wait_send()


VMEM = pl.BlockSpec(memory_space=pltpu.VMEM)


def on_device(tasks, task_owner, task_slot, p_pattern, c_pattern, occupations):
    count = tasks.shape[0]
    packed = pl.pallas_call(
        pack_kernel,
        out_shape=jax.ShapeDtypeStruct((2 * count, 2176), BF16),
        in_specs=[VMEM] * 4,
        out_specs=VMEM,
        compiler_params=pltpu.CompilerParams(vmem_limit_bytes=40 << 20),
        name="pack",
    )(tasks, task_owner, task_owner.reshape(1, count), task_slot.reshape(count, 1))
    got = lax.all_to_all(packed, ("row", "col"), split_axis=0, concat_axis=0, tiled=True)
    density = pl.pallas_call(
        assemble_kernel,
        out_shape=jax.ShapeDtypeStruct((2, 256, 512), BF16),
        in_specs=[VMEM] * 3,
        out_specs=VMEM,
        scratch_shapes=[pltpu.VMEM((512, 512), F32)],
        compiler_params=pltpu.CompilerParams(vmem_limit_bytes=40 << 20),
        name="assemble",
    )(got, p_pattern, occupations.reshape(8, BLK))
    dma = pltpu.SemaphoreType.DMA
    return pl.pallas_call(
        step_kernel,
        out_shape=jax.ShapeDtypeStruct((256, 1024), F32),
        in_specs=[VMEM] * 2,
        out_specs=VMEM,
        scratch_shapes=[
            pltpu.VMEM((8, 8, 256, 256), BF16),
            pltpu.VMEM((2, 4, 256, 512), BF16),
            pltpu.VMEM((2, 4, 256, 512), BF16),
            pltpu.VMEM((8, 256, 512), F32),
            pltpu.VMEM((2, 256, 512), F32),
            pltpu.VMEM((2, 2, 2, 256, 512), BF16),
            pltpu.VMEM((2, 2, 256, 512), BF16),
            pltpu.VMEM((2, 2, 2, 256, 512), BF16),
            pltpu.VMEM((2, 2, 256, 512), BF16),
            pltpu.VMEM((2, 256, 512), BF16),
            pltpu.VMEM((2, 128, 512), BF16),
            dma((3,)),
            dma((4,)),
            dma((4,)),
            dma((8,)),
            dma((8,)),
            dma((9,)),
            dma((9,)),
            dma((8,)),
            dma((8,)),
            dma((12,)),
            dma((12,)),
            dma,
            dma,
        ],
        compiler_params=pltpu.CompilerParams(
            vmem_limit_bytes=56 << 20, collective_id=0, has_side_effects=True
        ),
        name="purify",
    )(density, c_pattern)


def solution(mesh):
    return jax.shard_map(
        on_device,
        mesh=mesh,
        in_specs=(
            P(("row", "col"), None),
            P(("row", "col"), None),
            P(("row", "col")),
            P("row", "col"),
            P("row", "col"),
            P("row"),
        ),
        out_specs=P(("row", "layer"), "col"),
        check_vma=False,
    )
```

```python
import functools

import jax
import jax.numpy as jnp
from jax import lax
from jax.experimental import pallas as pl
from jax.experimental.pallas import tpu as pltpu
from jax.sharding import PartitionSpec as P

BLK = 64
HALF = 32
MESH = pl.DeviceIdType.MESH
BF16 = jnp.bfloat16
F32 = jnp.float32


def iota(shape, axis):
    return lax.broadcasted_iota(jnp.int32, shape, axis)


def dot(a, b):
    return jnp.dot(a, b, preferred_element_type=F32)


def pack_kernel(task_ref, owner_col_ref, owner_row_ref, slot_ref, out_ref):
    count = task_ref.shape[0]
    half = lax.axis_index("layer")
    earlier = iota((count, count), 0) < iota((count, count), 1)
    same = (owner_col_ref[...] == owner_row_ref[...]) & earlier
    placed = jnp.sum(same.astype(jnp.int32), axis=0, keepdims=True)
    target = owner_row_ref[...] * 2 + placed
    put = (iota((2 * count, count), 0) == target).astype(BF16)
    lane = iota((256, 128), 0)
    want = iota((256, 128), 1)
    source = (want // HALF) * BLK + half * HALF + want % HALF
    pick = (lane == source).astype(BF16)
    for group in range(task_ref.shape[1] // 256):
        piece = dot(task_ref[:, group * 256 : (group + 1) * 256], pick).astype(BF16)
        out_ref[:, group * 128 : (group + 1) * 128] = dot(put, piece).astype(BF16)
    slot = slot_ref[...]
    order = (slot % 16) * 8 + slot // 16
    marks = jnp.broadcast_to(order + 1, (count, 128)).astype(BF16)
    out_ref[:, 2048:2176] = (dot(put, marks) - 1.0).astype(BF16)


def assemble_kernel(got_ref, pattern_ref, occ_ref, out_ref, rows):
    row_id = lax.axis_index("row") * 512
    col_id = lax.axis_index("col") * 1024 + lax.axis_index("layer") * HALF
    entries = got_ref.shape[0]
    marks = (got_ref[:, 2048:2176].astype(F32) == iota((entries, 128), 1).astype(F32)).astype(BF16)
    spread = (iota((16, 512), 0) == iota((16, 512), 1) // HALF).astype(F32)
    mask = dot(pattern_ref[...].astype(F32), spread)
    column = col_id + (iota((8, 512), 1) // HALF) * BLK + iota((8, 512), 1) % HALF
    first = row_id + iota((8, 512), 0) * BLK
    quarter = iota((8, 128), 1) // HALF
    for quad in range(16):
        summed = lax.dot_general(
            marks,
            got_ref[:, quad * 128 : (quad + 1) * 128],
            (((0,), (0,)), ((), ())),
            preferred_element_type=F32,
        )
        for e in range(4):
            tiles = []
            for t in range(4):
                tile = None
                for f in range(4):
                    block = t * 4 + f
                    value = summed[block * 8 : (block + 1) * 8, :]
                    shift = (f - e) % 4
                    if shift:
                        value = pltpu.roll(value, shift * HALF, 1)
                    tile = value if tile is None else jnp.where(quarter == f, value, tile)
                tiles.append(tile)
            i = quad * 4 + e
            line = jnp.concatenate(tiles, axis=1) * mask
            line = line + jnp.where(first + i == column, occ_ref[:, i : i + 1], 0.0)
            rows[i * 8 : (i + 1) * 8, :] = line
    want = iota((256, 256), 0)
    have = iota((256, 256), 1)
    move = (have == (want % HALF) * 8 + want // HALF).astype(BF16)
    for h in range(2):
        moved = dot(move, rows[h * 256 : (h + 1) * 256, :].astype(BF16)).astype(BF16)
        out_ref[h] = moved.reshape(2, 2, 64, 512)


def step_kernel(
    d_ref, pattern_ref, out_ref,
    a, b, b2, acc, keep, low, near, far, near_in, far_in, result, swapped,
    local_sem, y_send, y_recv, z_send, z_recv, twin_send, twin_recv,
    x_send, x_recv, r_send, r_recv, swap_send, swap_recv,
):
    row, col, layer = lax.axis_index("row"), lax.axis_index("col"), lax.axis_index("layer")
    x, y = row // 4, row % 4
    core = col % 2
    z = layer * 4 + col // 2

    def device(xx, yy, zz, cc):
        return (xx * 4 + yy, (zz % 4) * 2 + cc, zz // 4)

    def ring(value, step, size):
        return (value + step + size) % size

    twin = device(x, y, z, 1 - core)
    up_y, down_y = device(x, ring(y, 1, 4), z, core), device(x, ring(y, -1, 4), z, core)
    up_x, down_x = device(ring(x, 1, 4), y, z, core), device(ring(x, -1, 4), y, z, core)
    up_z, down_z = device(x, y, ring(z, 1, 8), core), device(x, y, ring(z, -1, 8), core)
    across = device(x, y, ring(z, 4, 8), core)

    barrier = pltpu.get_barrier_semaphore()
    others = [device(x, ring(y, s, 4), z, c) for s in range(1, 4) for c in range(2)]
    others += [twin, up_x, down_x, up_z, down_z, across]
    for other in others:
        pl.semaphore_signal(barrier, inc=1, device_id=other, device_id_type=MESH)
    pl.semaphore_wait(barrier, len(others))

    sent = []

    def remote(src, dst, send, recv, to):
        return pltpu.make_async_remote_copy(
            src_ref=src, dst_ref=dst, send_sem=send, recv_sem=recv, device_id=to, device_id_type=MESH
        )

    def launch(src, dst, send, recv, to):
        copy = remote(src, dst, send, recv, to)
        copy.start()
        sent.append(copy)
        return copy

    y_copies = []
    for q in range(4):
        for p in range(2):
            for c in range(2):
                to_y = 2 * core + p
                mine = jnp.logical_and(to_y == y, core == c)
                src = d_ref.at[q // 2, q % 2, c, :, pl.ds(p * 256, 256)]
                dst = a.at[z, q, y, c]
                copy = remote(src, dst, y_send.at[q * 4 + p * 2 + c], y_recv.at[q, y], device(x, to_y, z, c))
                own = pltpu.make_async_copy(src, dst, local_sem.at[q])

                @pl.when(jnp.logical_not(mine))
                def _():
                    copy.start()

                @pl.when(mine)
                def _():
                    own.start()

                y_copies.append((mine, copy))

    def x_first(source, panel, sems, home_sem):
        mine = panel(x)
        up = launch(source, mine, x_send.at[sems], x_recv.at[sems], up_x)
        down = launch(source, mine, x_send.at[sems + 1], x_recv.at[sems + 1], down_x)
        home = pltpu.make_async_copy(source, mine, local_sem.at[home_sem])
        home.start()
        return up, down, home

    x_one = x_first(d_ref, lambda xx: b.at[:, xx], 0, 4)

    def x_second(pieces, sems, first):
        first[0].wait_recv()
        ref = pieces(ring(x, -1, 4), 0)
        up = launch(ref, ref, x_send.at[sems + 2], x_recv.at[sems + 2], up_x)
        first[1].wait_recv()
        ref = pieces(ring(x, 1, 4), 1)
        down = launch(ref, ref, x_send.at[sems + 3], x_recv.at[sems + 3], down_x)
        return up, down

    def y_arrived(q):
        for source_y in range(4):
            mine = jnp.logical_and(y == source_y, core == y // 2)
            block = a.at[z, q, source_y, core]

            @pl.when(jnp.logical_not(mine))
            def _():
                remote(block, block, y_send.at[0], y_recv.at[q, source_y], twin).wait_recv()

            @pl.when(mine)
            def _():
                pltpu.make_async_copy(block, block, local_sem.at[q]).wait()

    z_copies = {}

    def blocks(q, step):
        if step == 4:
            return ((ring(z, -4, 8), 0, 2), (ring(z, 4, 8), 2, 2))
        return ((ring(z, -step, 8), 0, 4), (ring(z, step, 8), 0, 4))

    def z_issue(q, step):
        (up_block, _, _), (down_block, _, _) = blocks(q, step - 1)
        size = 4 if step < 4 else 2
        index = q * 8 + (step - 1) * 2
        ref = a.at[up_block, q, pl.ds(0, size), core]
        up = launch(ref, ref, z_send.at[index], z_recv.at[index], up_z)
        ref = a.at[down_block, q, pl.ds(4 - size, size), core]
        down = launch(ref, ref, z_send.at[index + 1], z_recv.at[index + 1], down_z)
        z_copies[q, step] = (up, down)

    def twin_refs(q, step, side):
        if step == 0:
            return [(q * 9, a.at[z, q, :, side])]
        return [
            (q * 9 + step * 2 - 1 + k, a.at[block, q, pl.ds(low_y, size), side])
            for k, (block, low_y, size) in enumerate(blocks(q, step))
        ]

    def hand_over(q, step):
        for index, ref in twin_refs(q, step, core):
            launch(ref, ref, twin_send.at[index], twin_recv.at[index], twin)

    def z_arrived(q, step):
        for copy in z_copies[q, step]:
            copy.wait_recv()
        hand_over(q, step)

    def product(q, parts, first):
        def body(m, carry):
            total = None
            for zz, piece in parts:
                left = a[zz, q, pl.ds(2 * m, 2)].reshape(256, 256)
                term = dot(left, piece[...].reshape(256, 512))
                total = term if total is None else total + term
            total = total.reshape(2, 2, 64, 512)
            at = pl.ds(2 * m, 2)
            acc[q, at] = total if first else acc[q, at] + total
            return carry

        lax.fori_loop(0, 2, body, 0)

    r_copies = {}
    up_t, down_t, far_t = ring(y, 1, 4), ring(y, -1, 4), ring(y, 2, 4)

    def reduce_issue(n, k, q):
        base = (n * 4 + k) * 6

        def send(j, src, dst, to):
            r_copies[n, k, j] = launch(src, dst, r_send.at[base + j], r_recv.at[base + j], to)

        for side, to in ((0, up_y), (1, down_y)):
            far[n, k, side] = acc[q, far_t, side].astype(BF16)
            send(side, far.at[n, k, side], far_in.at[n, k, side], to)
        for side, t, to in ((0, up_t, up_y), (1, down_t, down_y)):
            near[n, k, side, 1 - side] = acc[q, t, 1 - side].astype(BF16)
            send(2 + side, near.at[n, k, side, 1 - side], near_in.at[n, k, side, 1 - side], to)

    def reduce_pass(n, k, q):
        base = (n * 4 + k) * 6
        for side, t, to in ((0, up_t, up_y), (1, down_t, down_y)):
            r_copies[n, k, side].wait_recv()
            near[n, k, side, side] = (acc[q, t, side] + far_in[n, k, side].astype(F32)).astype(BF16)
            r_copies[n, k, 4 + side] = launch(
                near.at[n, k, side, side], near_in.at[n, k, side, side],
                r_send.at[base + 4 + side], r_recv.at[base + 4 + side], to,
            )

    def reduce_end(n, k, q):
        for j in range(2, 6):
            r_copies[n, k, j].wait_recv()
        return acc[q, y] + near_in[n, k, 0].astype(F32) + near_in[n, k, 1].astype(F32)

    x_copies = {}

    def gather_issue(q):
        value = reduce_end(0, q, q)
        keep[q] = value
        low[q] = value.astype(BF16)
        x_copies[q] = x_first(low.at[q], lambda xx: b2.at[q // 2, xx, q % 2], 4 + 4 * q, 5 + q)

    def gather_pass(q):
        x_copies[q] += x_second(lambda xx, s: b2.at[q // 2, xx, q % 2, s], 4 + 4 * q, x_copies[q])

    def gather_end(q):
        x_copies[q][2].wait()
        for copy in x_copies[q][3:]:
            copy.wait_recv()

    def all_arrived(q):
        for step in range(5):
            for index, ref in twin_refs(q, step, 1 - core):
                remote(ref, ref, twin_send.at[index], twin_recv.at[index], twin).wait_recv()

    def square(q):
        all_arrived(q)
        product(q, [(zz, b.at[zz // 4, zz % 4]) for zz in range(8)], True)
        reduce_issue(0, q, q)

    for q in range(4):
        y_arrived(q)
        hand_over(q, 0)
        if q < 2:
            z_issue(q, 1)
    z_arrived(0, 1)
    z_issue(0, 2)
    z_arrived(1, 1)
    z_issue(1, 2)
    z_arrived(0, 2)
    z_issue(0, 3)
    z_arrived(1, 2)
    z_issue(1, 3)
    x_two = x_second(lambda xx, s: b.at[s, xx], 0, x_one)
    z_arrived(0, 3)
    z_issue(0, 4)
    z_arrived(1, 3)
    z_issue(2, 1)
    z_arrived(0, 4)
    z_issue(1, 4)
    for copy in x_two:
        copy.wait_recv()
    x_one[2].wait()
    square(0)
    z_arrived(2, 1)
    z_issue(3, 1)
    z_arrived(1, 4)
    z_issue(2, 2)
    square(1)
    reduce_pass(0, 0, 0)
    z_arrived(3, 1)
    z_issue(3, 2)
    gather_issue(0)
    reduce_pass(0, 1, 1)
    z_arrived(2, 2)
    z_issue(2, 3)
    gather_issue(1)
    gather_pass(0)
    z_arrived(3, 2)
    z_issue(3, 3)
    gather_pass(1)
    z_arrived(2, 3)
    z_issue(2, 4)
    gather_end(0)
    gather_end(1)
    z_arrived(3, 3)
    z_issue(3, 4)
    z_arrived(2, 4)
    square(2)
    z_arrived(3, 4)
    square(3)
    reduce_pass(0, 2, 2)
    reduce_pass(0, 3, 3)
    for q in range(2):
        product(q, [(zz, b2.at[0, zz]) for zz in range(4)], True)
    gather_issue(2)
    gather_issue(3)
    for q in range(2, 4):
        product(q, [(zz, b2.at[0, zz]) for zz in range(4)], True)
    gather_pass(2)
    gather_pass(3)
    gather_end(2)
    gather_end(3)
    order = [1 - layer, 3 - layer, layer, 2 + layer]
    for k, q in enumerate(order):
        product(q, [(4 + zz, b2.at[1, zz]) for zz in range(4)], False)
        reduce_issue(1, k, q)
    swaps = []
    spread = (iota((16, 1024), 0) == iota((16, 1024), 1) // BLK).astype(F32)
    mask_all = dot(pattern_ref[...].astype(F32), spread)
    mask = jnp.where(layer == 0, mask_all[0:4], mask_all[4:8])
    source = iota((256, 256), 0)
    want = iota((256, 256), 1)
    side = jnp.where(source < 128, layer, 1 - layer)
    goes = ((source % 128) // HALF) * BLK + side * HALF + source % HALF
    place = (goes == want).astype(BF16)

    def finish(k):
        q = order[k]
        result[k] = (3.0 * keep[q] - 2.0 * reduce_end(1, k, q)).astype(BF16)
        if k < 2:
            swaps.append(launch(result.at[k], swapped.at[k], swap_send.at[k], swap_recv.at[k], across))
            return
        half = k - 2
        swaps[half].wait_recv()
        own = result[k].reshape(128, 512)
        other = swapped[half].reshape(128, 512)
        for t in range(4):
            both = jnp.concatenate([own[:, t * 128 : (t + 1) * 128], other[:, t * 128 : (t + 1) * 128]], axis=1)
            full = dot(both, place)
            for blk in range(4):
                out_ref[blk * BLK + half * HALF : blk * BLK + (half + 1) * HALF, t * 256 : (t + 1) * 256] = (
                    full[blk * HALF : (blk + 1) * HALF] * mask[blk : blk + 1, t * 256 : (t + 1) * 256]
                )

    for k, q in enumerate(order):
        reduce_pass(1, k, q)
        if k >= 1:
            finish(k - 1)
    finish(3)

    for mine, copy in y_copies:
        @pl.when(jnp.logical_not(mine))
        def _():
            copy.wait_send()

    for copy in sent:
        copy.wait_send()


VMEM = pl.BlockSpec(memory_space=pltpu.VMEM)


def on_device(tasks, task_owner, task_slot, p_pattern, c_pattern, occupations):
    count = tasks.shape[0]
    packed = pl.pallas_call(
        pack_kernel,
        out_shape=jax.ShapeDtypeStruct((2 * count, 2176), BF16),
        in_specs=[VMEM] * 4,
        out_specs=VMEM,
        compiler_params=pltpu.CompilerParams(vmem_limit_bytes=40 << 20),
        name="pack",
    )(tasks, task_owner, task_owner.reshape(1, count), task_slot.reshape(count, 1))
    got = lax.all_to_all(packed, ("row", "col"), split_axis=0, concat_axis=0, tiled=True)
    density = pl.pallas_call(
        assemble_kernel,
        out_shape=jax.ShapeDtypeStruct((2, 2, 2, 64, 512), BF16),
        in_specs=[VMEM] * 3,
        out_specs=VMEM,
        scratch_shapes=[pltpu.VMEM((512, 512), F32)],
        compiler_params=pltpu.CompilerParams(vmem_limit_bytes=40 << 20),
        name="assemble",
    )(got, p_pattern, occupations.reshape(8, BLK))
    dma = pltpu.SemaphoreType.DMA
    return pl.pallas_call(
        step_kernel,
        out_shape=jax.ShapeDtypeStruct((256, 1024), F32),
        in_specs=[VMEM] * 2,
        out_specs=VMEM,
        scratch_shapes=[
            pltpu.VMEM((8, 4, 4, 2, 64, 256), BF16),
            pltpu.VMEM((2, 4, 2, 2, 64, 512), BF16),
            pltpu.VMEM((2, 4, 2, 2, 64, 512), BF16),
            pltpu.VMEM((4, 4, 2, 64, 512), F32),
            pltpu.VMEM((4, 2, 64, 512), F32),
            pltpu.VMEM((4, 2, 64, 512), BF16),
            pltpu.VMEM((2, 4, 2, 2, 64, 512), BF16),
            pltpu.VMEM((2, 4, 2, 64, 512), BF16),
            pltpu.VMEM((2, 4, 2, 2, 64, 512), BF16),
            pltpu.VMEM((2, 4, 2, 64, 512), BF16),
            pltpu.VMEM((4, 2, 64, 512), BF16),
            pltpu.VMEM((2, 2, 64, 512), BF16),
            dma((9,)),
            dma((16,)),
            dma((4, 4)),
            dma((32,)),
            dma((32,)),
            dma((36,)),
            dma((36,)),
            dma((20,)),
            dma((20,)),
            dma((48,)),
            dma((48,)),
            dma((2,)),
            dma((2,)),
        ],
        compiler_params=pltpu.CompilerParams(
            vmem_limit_bytes=56 << 20, collective_id=0, has_side_effects=True
        ),
        name="purify",
    )(density, c_pattern)


def solution(mesh):
    return jax.shard_map(
        on_device,
        mesh=mesh,
        in_specs=(
            P(("row", "col"), None),
            P(("row", "col"), None),
            P(("row", "col")),
            P("row", "col"),
            P("row", "col"),
            P("row"),
        ),
        out_specs=P(("row", "layer"), "col"),
        check_vma=False,
    )
```

```python
import functools

import jax
import jax.numpy as jnp
from jax import lax
from jax.experimental import pallas as pl
from jax.experimental.pallas import tpu as pltpu
from jax.sharding import PartitionSpec as P

BLK = 64
HALF = 32
MESH = pl.DeviceIdType.MESH
BF16 = jnp.bfloat16
F32 = jnp.float32


def iota(shape, axis):
    return lax.broadcasted_iota(jnp.int32, shape, axis)


def dot(a, b):
    return jnp.dot(a, b, preferred_element_type=F32)


UNITS = ((0, 0, 2), (1, 2, 2), (-1, 4, 2), (2, 6, 1), (-2, 7, 1))


def z_shift(unit):
    near_by = jnp.where(unit < 2, 0, jnp.where(unit < 4, 1, -1))
    return jnp.where(unit == 6, 2, jnp.where(unit == 7, -2, near_by))


def pack(task_ref, owner_ref, slot_ref, z, wide, packed, info):
    count = task_ref.shape[0]
    owner = owner_ref[...]
    column = jnp.transpose(jnp.broadcast_to(owner.astype(F32), (count, count))).astype(jnp.int32)
    earlier = iota((count, count), 0) < iota((count, count), 1)
    placed = jnp.sum(jnp.logical_and(column == owner, earlier).astype(jnp.int32), axis=0, keepdims=True)
    line = iota((256, count), 0)
    unit = line % 8
    there = (z + z_shift(unit) + 8) % 8
    wanted = (((line // 8) % 4) * 4 + (line // 32) % 4) * 8 + (there % 4) * 2 + line // 128
    put = jnp.logical_and(owner == wanted, placed == unit % 2)
    halves = jnp.concatenate(
        [jnp.logical_and(put, there // 4 == h).astype(F32) for h in range(2)], axis=1
    ).astype(BF16)
    lane = iota((256, 256), 0)
    goes = iota((256, 256), 1)
    source = ((goes % 128) // HALF) * BLK + (goes // 128) * HALF + goes % HALF
    pick = (lane == source).astype(BF16)
    for p in range(16):
        piece = dot(task_ref[:, p * 256 : (p + 1) * 256], pick).astype(BF16)
        both = jnp.concatenate([piece[:, :128], piece[:, 128:]], axis=0)
        wide[pl.ds(p, 256, stride=16), :] = dot(halves, both)
    for part in range(16):
        value = wide[part * 256 : (part + 1) * 256, :].astype(BF16)
        packed[part // 8, (part % 8) * 2 : (part % 8) * 2 + 2] = value.reshape(2, 8, 16, 128)
    slot = slot_ref[...]
    order = (slot % 16) * 8 + slot // 16 + 1
    mark = jnp.sum(jnp.where(put, order, 0).astype(F32), axis=1, keepdims=True)
    at = iota((256, 128), 1) == iota((256, 128), 0) // 8
    rows = (iota((8, 256), 0) == iota((8, 256), 1) % 8).astype(BF16)
    info[0] = dot(rows, jnp.where(at, mark, 0.0).astype(BF16)) - 1.0


def assemble(got, info, lane, row_id, col_id, pattern_ref, occ_ref, wide, rows, out_ref):
    tiles = [info[k].reshape(128, 128) for k in range(2)]
    tiles = jnp.concatenate(tiles, axis=0)
    slot = jnp.sum(jnp.where(iota((256, 128), 1) == lane, tiles, 0.0), axis=1, keepdims=True)
    marks = jnp.where(slot == iota((256, 128), 1).astype(F32), 1.0, 0.0)
    marks = jnp.transpose(marks).astype(BF16)
    for part in range(16):
        value = got[part // 8, (part % 8) * 2 : (part % 8) * 2 + 2]
        wide[part * 256 : (part + 1) * 256, :] = value.reshape(256, 128).astype(F32)
    spread = (iota((16, 512), 0) == iota((16, 512), 1) // HALF).astype(F32)
    mask = dot(pattern_ref[...].astype(F32), spread)
    column = col_id + (iota((8, 512), 1) // HALF) * BLK + iota((8, 512), 1) % HALF
    first = row_id + iota((8, 512), 0) * BLK
    quarter = iota((8, 128), 1) // HALF
    for quad in range(16):
        summed = dot(marks, wide[pl.ds(quad, 256, stride=16), :].astype(BF16))
        for e in range(4):
            tiles = []
            for t in range(4):
                tile = None
                for f in range(4):
                    block = t * 4 + f
                    value = summed[block * 8 : (block + 1) * 8, :]
                    shift = (f - e) % 4
                    if shift:
                        value = pltpu.roll(value, shift * HALF, 1)
                    tile = value if tile is None else jnp.where(quarter == f, value, tile)
                tiles.append(tile)
            i = quad * 4 + e
            line = jnp.concatenate(tiles, axis=1) * mask
            line = line + jnp.where(first + i == column, occ_ref[:, i : i + 1], 0.0)
            rows[i * 8 : (i + 1) * 8, :] = line
    want = iota((256, 256), 0)
    have = iota((256, 256), 1)
    move = (have == (want % HALF) * 8 + want // HALF).astype(BF16)
    for h in range(2):
        moved = dot(move, rows[h * 256 : (h + 1) * 256, :].astype(BF16)).astype(BF16)
        out_ref[h] = moved.reshape(2, 2, 64, 512)


def step_kernel(
    task_ref, owner_ref, slot_ref, p_pattern_ref, occ_ref, pattern_ref, out_ref,
    wide, packed, by_z, twin_in, by_xy, got, info, info_z, info_xy, rows, d_ref,
    t_local, t_send, t_recv, a, b, b2, acc, keep, low, near, far, near_in, far_in, result, swapped,
    local_sem, y_send, y_recv, z_send, z_recv, twin_send, twin_recv,
    x_send, x_recv, r_send, r_recv, swap_send, swap_recv,
):
    row, col, layer = lax.axis_index("row"), lax.axis_index("col"), lax.axis_index("layer")
    x, y = row // 4, row % 4
    core = col % 2
    z = layer * 4 + col // 2

    def device(xx, yy, zz, cc):
        return (xx * 4 + yy, (zz % 4) * 2 + cc, zz // 4)

    def ring(value, step, size):
        return (value + step + size) % size

    twin = device(x, y, z, 1 - core)
    up_y, down_y = device(x, ring(y, 1, 4), z, core), device(x, ring(y, -1, 4), z, core)
    up_x, down_x = device(ring(x, 1, 4), y, z, core), device(ring(x, -1, 4), y, z, core)
    up_z, down_z = device(x, y, ring(z, 1, 8), core), device(x, y, ring(z, -1, 8), core)
    across = device(x, y, ring(z, 4, 8), core)

    barrier = pltpu.get_barrier_semaphore()
    others = [device(x, ring(y, s, 4), z, 1 - core) for s in range(1, 4)]
    spot = y * 4 + x
    plane = [(spot + s) % 16 for s in range(1, 16)]
    others += [device(at % 4, at // 4, z, core) for at in plane]
    others += [twin, across] + [device(x, y, ring(z, s, 8), core) for s in (1, -1, 2, -2)]
    for other in others:
        pl.semaphore_signal(barrier, inc=1, device_id=other, device_id_type=MESH)
    pack(task_ref, owner_ref, slot_ref, z, wide, packed, info)
    pl.semaphore_wait(barrier, len(others))

    sent = []

    def remote(src, dst, send, recv, to):
        return pltpu.make_async_remote_copy(
            src_ref=src, dst_ref=dst, send_sem=send, recv_sem=recv, device_id=to, device_id_type=MESH
        )

    def launch(src, dst, send, recv, to):
        copy = remote(src, dst, send, recv, to)
        copy.start()
        sent.append(copy)
        return copy

    def home(src, dst, index):
        copy = pltpu.make_async_copy(src, dst, t_local.at[index])
        copy.start()
        return copy

    def over_z(source, target, base, own):
        copies = []
        for index, (shift, low_unit, size) in enumerate(UNITS[1:]):
            units = pl.ds(low_unit, size)
            to = device(x, y, ring(z, shift, 8), core)
            at = base + index
            copies.append(launch(source.at[:, units], target.at[:, units], t_send.at[at], t_recv.at[at], to))
        return copies, home(source.at[:, pl.ds(0, 2)], target.at[:, pl.ds(0, 2)], own)

    def over_plane(source, target, recv, base, own):
        for index, at in enumerate(plane):
            to = device(at % 4, at // 4, z, core)
            launch(source(at), target.at[spot], t_send.at[base + index], t_recv.at[recv], to)
        copy = home(source(spot), target.at[spot], own)
        several = target.at[pl.ds(0, 15)]

        def arrived():
            remote(several, several, t_send.at[0], t_recv.at[recv], twin).wait_recv()
            copy.wait()

        return arrived

    info_copies = []
    for index, (shift, _, _) in enumerate(UNITS[1:]):
        to = device(x, y, ring(z, shift, 8), core)
        info_copies.append(launch(info.at[0], info_z.at[index], t_send.at[index], t_recv.at[index], to))
    to_twin = launch(packed.at[1 - core], twin_in, t_send.at[4], t_recv.at[4], twin)
    z_tasks, z_home = over_z(packed.at[core], by_z, 5, 0)
    to_twin.wait_recv()
    plane_b = over_plane(lambda at: twin_in.at[at], by_xy, 13, 13, 1)
    for copy in info_copies:
        copy.wait_recv()
    unit = iota((8, 128), 0)
    merged = info[0]
    for index, (_, low_unit, size) in enumerate(UNITS[1:]):
        fits = jnp.logical_and(unit >= low_unit, unit < low_unit + size)
        merged = jnp.where(fits, info_z[index], merged)
    info[1] = merged
    plane_i = over_plane(lambda at: info.at[1], info_xy.at[0], 14, 28, 2)
    for copy in z_tasks:
        copy.wait_recv()
    z_home.wait()
    plane_a = over_plane(lambda at: by_z.at[at], got.at[0], 15, 43, 3)
    plane_b()
    z_more, z_more_home = over_z(by_xy, got.at[1], 9, 4)
    plane_i()
    twin_info = launch(info_xy.at[0], info_xy.at[1], t_send.at[58], t_recv.at[16], twin)
    plane_a()
    twin_info.wait_recv()
    for copy in z_more:
        copy.wait_recv()
    z_more_home.wait()
    assemble(
        got, info_xy, core * 16 + spot, row * 512, col * 1024 + layer * HALF,
        p_pattern_ref, occ_ref, wide, rows, d_ref,
    )

    y_copies = []
    for q in range(4):
        for p in range(2):
            for c in range(2):
                to_y = 2 * core + p
                mine = jnp.logical_and(to_y == y, core == c)
                src = d_ref.at[q // 2, q % 2, c, :, pl.ds(p * 256, 256)]
                dst = a.at[z, q, y, c]
                copy = remote(src, dst, y_send.at[q * 4 + p * 2 + c], y_recv.at[q, y], device(x, to_y, z, c))
                own = pltpu.make_async_copy(src, dst, local_sem.at[q])

                @pl.when(jnp.logical_not(mine))
                def _():
                    copy.start()

                @pl.when(mine)
                def _():
                    own.start()

                y_copies.append((mine, copy))

    def x_first(source, panel, sems, home_sem):
        mine = panel(x)
        up = launch(source, mine, x_send.at[sems], x_recv.at[sems], up_x)
        down = launch(source, mine, x_send.at[sems + 1], x_recv.at[sems + 1], down_x)
        home = pltpu.make_async_copy(source, mine, local_sem.at[home_sem])
        home.start()
        return up, down, home

    x_one = x_first(d_ref, lambda xx: b.at[:, xx], 0, 4)

    def x_second(pieces, sems, first):
        first[0].wait_recv()
        ref = pieces(ring(x, -1, 4), 0)
        up = launch(ref, ref, x_send.at[sems + 2], x_recv.at[sems + 2], up_x)
        first[1].wait_recv()
        ref = pieces(ring(x, 1, 4), 1)
        down = launch(ref, ref, x_send.at[sems + 3], x_recv.at[sems + 3], down_x)
        return up, down

    def y_arrived(q):
        for source_y in range(4):
            mine = jnp.logical_and(y == source_y, core == y // 2)
            block = a.at[z, q, source_y, core]

            @pl.when(jnp.logical_not(mine))
            def _():
                remote(block, block, y_send.at[0], y_recv.at[q, source_y], twin).wait_recv()

            @pl.when(mine)
            def _():
                pltpu.make_async_copy(block, block, local_sem.at[q]).wait()

    z_copies = {}

    def blocks(q, step):
        if step == 4:
            return ((ring(z, -4, 8), 0, 2), (ring(z, 4, 8), 2, 2))
        return ((ring(z, -step, 8), 0, 4), (ring(z, step, 8), 0, 4))

    def z_issue(q, step):
        (up_block, _, _), (down_block, _, _) = blocks(q, step - 1)
        size = 4 if step < 4 else 2
        index = q * 8 + (step - 1) * 2
        ref = a.at[up_block, q, pl.ds(0, size), core]
        up = launch(ref, ref, z_send.at[index], z_recv.at[index], up_z)
        ref = a.at[down_block, q, pl.ds(4 - size, size), core]
        down = launch(ref, ref, z_send.at[index + 1], z_recv.at[index + 1], down_z)
        z_copies[q, step] = (up, down)

    def twin_refs(q, step, side):
        if step == 0:
            return [(q * 9, a.at[z, q, :, side])]
        return [
            (q * 9 + step * 2 - 1 + k, a.at[block, q, pl.ds(low_y, size), side])
            for k, (block, low_y, size) in enumerate(blocks(q, step))
        ]

    def hand_over(q, step):
        for index, ref in twin_refs(q, step, core):
            launch(ref, ref, twin_send.at[index], twin_recv.at[index], twin)

    def z_arrived(q, step):
        for copy in z_copies[q, step]:
            copy.wait_recv()
        hand_over(q, step)

    def product(q, parts, first):
        def body(m, carry):
            total = None
            for zz, piece in parts:
                left = a[zz, q, pl.ds(2 * m, 2)].reshape(256, 256)
                term = dot(left, piece[...].reshape(256, 512))
                total = term if total is None else total + term
            total = total.reshape(2, 2, 64, 512)
            at = pl.ds(2 * m, 2)
            acc[q, at] = total if first else acc[q, at] + total
            return carry

        lax.fori_loop(0, 2, body, 0)

    r_copies = {}
    up_t, down_t, far_t = ring(y, 1, 4), ring(y, -1, 4), ring(y, 2, 4)

    def reduce_issue(n, k, q):
        base = (n * 4 + k) * 6

        def send(j, src, dst, to):
            r_copies[n, k, j] = launch(src, dst, r_send.at[base + j], r_recv.at[base + j], to)

        for side, to in ((0, up_y), (1, down_y)):
            far[n, k, side] = acc[q, far_t, side].astype(BF16)
            send(side, far.at[n, k, side], far_in.at[n, k, side], to)
        for side, t, to in ((0, up_t, up_y), (1, down_t, down_y)):
            near[n, k, side, 1 - side] = acc[q, t, 1 - side].astype(BF16)
            send(2 + side, near.at[n, k, side, 1 - side], near_in.at[n, k, side, 1 - side], to)

    def reduce_pass(n, k, q):
        base = (n * 4 + k) * 6
        for side, t, to in ((0, up_t, up_y), (1, down_t, down_y)):
            r_copies[n, k, side].wait_recv()
            near[n, k, side, side] = (acc[q, t, side] + far_in[n, k, side].astype(F32)).astype(BF16)
            r_copies[n, k, 4 + side] = launch(
                near.at[n, k, side, side], near_in.at[n, k, side, side],
                r_send.at[base + 4 + side], r_recv.at[base + 4 + side], to,
            )

    def reduce_end(n, k, q):
        for j in range(2, 6):
            r_copies[n, k, j].wait_recv()
        return acc[q, y] + near_in[n, k, 0].astype(F32) + near_in[n, k, 1].astype(F32)

    x_copies = {}

    def gather_issue(q):
        value = reduce_end(0, q, q)
        keep[q] = value
        low[q] = value.astype(BF16)
        x_copies[q] = x_first(low.at[q], lambda xx: b2.at[q // 2, xx, q % 2], 4 + 4 * q, 5 + q)

    def gather_pass(q):
        x_copies[q] += x_second(lambda xx, s: b2.at[q // 2, xx, q % 2, s], 4 + 4 * q, x_copies[q])

    def gather_end(q):
        x_copies[q][2].wait()
        for copy in x_copies[q][3:]:
            copy.wait_recv()

    def all_arrived(q):
        for step in range(5):
            for index, ref in twin_refs(q, step, 1 - core):
                remote(ref, ref, twin_send.at[index], twin_recv.at[index], twin).wait_recv()

    def square(q):
        all_arrived(q)
        product(q, [(zz, b.at[zz // 4, zz % 4]) for zz in range(8)], True)
        reduce_issue(0, q, q)

    for q in range(4):
        y_arrived(q)
        hand_over(q, 0)
        if q < 2:
            z_issue(q, 1)
    z_arrived(0, 1)
    z_issue(0, 2)
    z_arrived(1, 1)
    z_issue(1, 2)
    z_arrived(0, 2)
    z_issue(0, 3)
    z_arrived(1, 2)
    z_issue(1, 3)
    x_two = x_second(lambda xx, s: b.at[s, xx], 0, x_one)
    z_arrived(0, 3)
    z_issue(0, 4)
    z_arrived(1, 3)
    z_issue(2, 1)
    z_arrived(0, 4)
    z_issue(1, 4)
    for copy in x_two:
        copy.wait_recv()
    x_one[2].wait()
    square(0)
    z_arrived(2, 1)
    z_issue(3, 1)
    z_arrived(1, 4)
    z_issue(2, 2)
    square(1)
    reduce_pass(0, 0, 0)
    z_arrived(3, 1)
    z_issue(3, 2)
    gather_issue(0)
    reduce_pass(0, 1, 1)
    z_arrived(2, 2)
    z_issue(2, 3)
    gather_issue(1)
    gather_pass(0)
    z_arrived(3, 2)
    z_issue(3, 3)
    gather_pass(1)
    z_arrived(2, 3)
    z_issue(2, 4)
    gather_end(0)
    gather_end(1)
    z_arrived(3, 3)
    z_issue(3, 4)
    z_arrived(2, 4)
    square(2)
    z_arrived(3, 4)
    square(3)
    reduce_pass(0, 2, 2)
    reduce_pass(0, 3, 3)
    for q in range(2):
        product(q, [(zz, b2.at[0, zz]) for zz in range(4)], True)
    gather_issue(2)
    gather_issue(3)
    for q in range(2, 4):
        product(q, [(zz, b2.at[0, zz]) for zz in range(4)], True)
    gather_pass(2)
    gather_pass(3)
    gather_end(2)
    gather_end(3)
    order = [1 - layer, 3 - layer, layer, 2 + layer]
    for k, q in enumerate(order):
        product(q, [(4 + zz, b2.at[1, zz]) for zz in range(4)], False)
        reduce_issue(1, k, q)
    swaps = []
    spread = (iota((16, 1024), 0) == iota((16, 1024), 1) // BLK).astype(F32)
    mask_all = dot(pattern_ref[...].astype(F32), spread)
    mask = jnp.where(layer == 0, mask_all[0:4], mask_all[4:8])
    source = iota((256, 256), 0)
    want = iota((256, 256), 1)
    side = jnp.where(source < 128, layer, 1 - layer)
    goes = ((source % 128) // HALF) * BLK + side * HALF + source % HALF
    place = (goes == want).astype(BF16)

    def finish(k):
        q = order[k]
        result[k] = (3.0 * keep[q] - 2.0 * reduce_end(1, k, q)).astype(BF16)
        if k < 2:
            swaps.append(launch(result.at[k], swapped.at[k], swap_send.at[k], swap_recv.at[k], across))
            return
        half = k - 2
        swaps[half].wait_recv()
        own = result[k].reshape(128, 512)
        other = swapped[half].reshape(128, 512)
        for t in range(4):
            both = jnp.concatenate([own[:, t * 128 : (t + 1) * 128], other[:, t * 128 : (t + 1) * 128]], axis=1)
            full = dot(both, place)
            for blk in range(4):
                out_ref[blk * BLK + half * HALF : blk * BLK + (half + 1) * HALF, t * 256 : (t + 1) * 256] = (
                    full[blk * HALF : (blk + 1) * HALF] * mask[blk : blk + 1, t * 256 : (t + 1) * 256]
                )

    for k, q in enumerate(order):
        reduce_pass(1, k, q)
        if k >= 1:
            finish(k - 1)
    finish(3)

    for mine, copy in y_copies:
        @pl.when(jnp.logical_not(mine))
        def _():
            copy.wait_send()

    for copy in sent:
        copy.wait_send()


VMEM = pl.BlockSpec(memory_space=pltpu.VMEM)


def on_device(tasks, task_owner, task_slot, p_pattern, c_pattern, occupations):
    dma = pltpu.SemaphoreType.DMA
    count = tasks.shape[0]
    return pl.pallas_call(
        step_kernel,
        out_shape=jax.ShapeDtypeStruct((256, 1024), F32),
        in_specs=[VMEM] * 6,
        out_specs=VMEM,
        scratch_shapes=[
            pltpu.VMEM((4096, 128), F32),
            pltpu.VMEM((2, 16, 8, 16, 128), BF16),
            pltpu.VMEM((16, 8, 16, 128), BF16),
            pltpu.VMEM((16, 8, 16, 128), BF16),
            pltpu.VMEM((16, 8, 16, 128), BF16),
            pltpu.VMEM((2, 16, 8, 16, 128), BF16),
            pltpu.VMEM((2, 8, 128), F32),
            pltpu.VMEM((4, 8, 128), F32),
            pltpu.VMEM((2, 16, 8, 128), F32),
            pltpu.VMEM((512, 512), F32),
            pltpu.VMEM((2, 2, 2, 64, 512), BF16),
            dma((5,)),
            dma((59,)),
            dma((17,)),
            pltpu.VMEM((8, 4, 4, 2, 64, 256), BF16),
            pltpu.VMEM((2, 4, 2, 2, 64, 512), BF16),
            pltpu.VMEM((2, 4, 2, 2, 64, 512), BF16),
            pltpu.VMEM((4, 4, 2, 64, 512), F32),
            pltpu.VMEM((4, 2, 64, 512), F32),
            pltpu.VMEM((4, 2, 64, 512), BF16),
            pltpu.VMEM((2, 4, 2, 2, 64, 512), BF16),
            pltpu.VMEM((2, 4, 2, 64, 512), BF16),
            pltpu.VMEM((2, 4, 2, 2, 64, 512), BF16),
            pltpu.VMEM((2, 4, 2, 64, 512), BF16),
            pltpu.VMEM((4, 2, 64, 512), BF16),
            pltpu.VMEM((2, 2, 64, 512), BF16),
            dma((9,)),
            dma((16,)),
            dma((4, 4)),
            dma((32,)),
            dma((32,)),
            dma((36,)),
            dma((36,)),
            dma((20,)),
            dma((20,)),
            dma((48,)),
            dma((48,)),
            dma((2,)),
            dma((2,)),
        ],
        compiler_params=pltpu.CompilerParams(
            vmem_limit_bytes=56 << 20, collective_id=0, has_side_effects=True
        ),
        name="purify",
    )(
        tasks, task_owner.reshape(1, count), task_slot.reshape(1, count), p_pattern,
        occupations.reshape(8, BLK), c_pattern,
    )


def solution(mesh):
    return jax.shard_map(
        on_device,
        mesh=mesh,
        in_specs=(
            P(("row", "col"), None),
            P(("row", "col"), None),
            P(("row", "col")),
            P("row", "col"),
            P("row", "col"),
            P("row"),
        ),
        out_specs=P(("row", "layer"), "col"),
        check_vma=False,
    )
```

```python
import functools

import jax
import jax.numpy as jnp
from jax import lax
from jax.experimental import pallas as pl
from jax.experimental.pallas import tpu as pltpu
from jax.sharding import PartitionSpec as P

BLK = 64
HALF = 32
MESH = pl.DeviceIdType.MESH
BF16 = jnp.bfloat16
F32 = jnp.float32


def iota(shape, axis):
    return lax.broadcasted_iota(jnp.int32, shape, axis)


def dot(a, b):
    return jnp.dot(a, b, preferred_element_type=F32)


UNITS = ((0, 0, 2), (1, 2, 2), (-1, 4, 2), (2, 6, 1), (-2, 7, 1))


def z_shift(unit):
    near_by = jnp.where(unit < 2, 0, jnp.where(unit < 4, 1, -1))
    return jnp.where(unit == 6, 2, jnp.where(unit == 7, -2, near_by))


def pack(task_ref, owner_ref, slot_ref, z, wide, packed, info):
    count = task_ref.shape[0]
    owner = owner_ref[...]
    column = jnp.transpose(jnp.broadcast_to(owner.astype(F32), (count, count))).astype(jnp.int32)
    earlier = iota((count, count), 0) < iota((count, count), 1)
    placed = jnp.sum(jnp.logical_and(column == owner, earlier).astype(jnp.int32), axis=0, keepdims=True)
    line = iota((256, count), 0)
    unit = line % 8
    there = (z + z_shift(unit) + 8) % 8
    wanted = (((line // 8) % 4) * 4 + (line // 32) % 4) * 8 + (there % 4) * 2 + line // 128
    put = jnp.logical_and(owner == wanted, placed == unit % 2)
    halves = jnp.concatenate(
        [jnp.logical_and(put, there // 4 == h).astype(F32) for h in range(2)], axis=1
    ).astype(BF16)
    lane = iota((256, 256), 0)
    goes = iota((256, 256), 1)
    source = ((goes % 128) // HALF) * BLK + (goes // 128) * HALF + goes % HALF
    pick = (lane == source).astype(BF16)
    for p in range(16):
        piece = dot(task_ref[:, p * 256 : (p + 1) * 256], pick).astype(BF16)
        both = jnp.concatenate([piece[:, :128], piece[:, 128:]], axis=0)
        wide[pl.ds(p, 256, stride=16), :] = dot(halves, both)
    for part in range(16):
        value = wide[part * 256 : (part + 1) * 256, :].astype(BF16)
        packed[part // 8, (part % 8) * 2 : (part % 8) * 2 + 2] = value.reshape(2, 8, 16, 128)
    slot = slot_ref[...]
    order = (slot % 16) * 8 + slot // 16 + 1
    mark = jnp.sum(jnp.where(put, order, 0).astype(F32), axis=1, keepdims=True)
    at = iota((256, 128), 1) == iota((256, 128), 0) // 8
    rows = (iota((8, 256), 0) == iota((8, 256), 1) % 8).astype(BF16)
    info[0] = dot(rows, jnp.where(at, mark, 0.0).astype(BF16)) - 1.0


def assemble(got, info, lane, row_id, col_id, pattern_ref, occ_ref, wide, rows, out_ref):
    tiles = [info[k].reshape(128, 128) for k in range(2)]
    tiles = jnp.concatenate(tiles, axis=0)
    slot = jnp.sum(jnp.where(iota((256, 128), 1) == lane, tiles, 0.0), axis=1, keepdims=True)
    marks = jnp.where(slot == iota((256, 128), 1).astype(F32), 1.0, 0.0)
    marks = jnp.transpose(marks).astype(BF16)
    for part in range(16):
        value = got[part // 8, (part % 8) * 2 : (part % 8) * 2 + 2]
        wide[part * 256 : (part + 1) * 256, :] = value.reshape(256, 128).astype(F32)
    spread = (iota((16, 512), 0) == iota((16, 512), 1) // HALF).astype(F32)
    mask = dot(pattern_ref[...].astype(F32), spread)
    column = col_id + (iota((8, 512), 1) // HALF) * BLK + iota((8, 512), 1) % HALF
    first = row_id + iota((8, 512), 0) * BLK
    quarter = iota((8, 128), 1) // HALF
    doubled = jnp.concatenate([occ_ref[r // 2 : r // 2 + 1, :] for r in range(8)], axis=0)
    occ = jnp.where(iota((8, 128), 0) % 2 == 0, doubled, pltpu.roll(doubled, BLK, 1))
    for quad in range(16):
        summed = dot(marks, wide[pl.ds(quad, 256, stride=16), :].astype(BF16))
        for e in range(4):
            tiles = []
            for t in range(4):
                tile = None
                for f in range(4):
                    block = t * 4 + f
                    value = summed[block * 8 : (block + 1) * 8, :]
                    shift = (f - e) % 4
                    if shift:
                        value = pltpu.roll(value, shift * HALF, 1)
                    tile = value if tile is None else jnp.where(quarter == f, value, tile)
                tiles.append(tile)
            i = quad * 4 + e
            line = jnp.concatenate(tiles, axis=1) * mask
            line = line + jnp.where(first + i == column, occ[:, i : i + 1], 0.0)
            rows[i * 8 : (i + 1) * 8, :] = line
    want = iota((256, 256), 0)
    have = iota((256, 256), 1)
    move = (have == (want % HALF) * 8 + want // HALF).astype(BF16)
    for h in range(2):
        moved = dot(move, rows[h * 256 : (h + 1) * 256, :].astype(BF16)).astype(BF16)
        out_ref[h] = moved.reshape(2, 2, 64, 512)


def step_kernel(
    task_ref, owner_ref, slot_ref, p_pattern_ref, occ_ref, own_ref, other_ref,
    wide, packed, by_z, by_xy, got, info, info_z, info_xy, rows, d_ref,
    t_local, t_send, t_recv, a, b, b2, acc, keep, low, near, far, near_in, far_in, result,
    local_sem, y_send, y_recv, z_send, z_recv, twin_send, twin_recv,
    x_send, x_recv, r_send, r_recv, swap_send, swap_recv,
):
    row, col, layer = lax.axis_index("row"), lax.axis_index("col"), lax.axis_index("layer")
    x, y = row // 4, row % 4
    core = col % 2
    z = layer * 4 + col // 2

    def device(xx, yy, zz, cc):
        return (xx * 4 + yy, (zz % 4) * 2 + cc, zz // 4)

    def ring(value, step, size):
        return (value + step + size) % size

    twin = device(x, y, z, 1 - core)
    up_y, down_y = device(x, ring(y, 1, 4), z, core), device(x, ring(y, -1, 4), z, core)
    up_x, down_x = device(ring(x, 1, 4), y, z, core), device(ring(x, -1, 4), y, z, core)
    up_z, down_z = device(x, y, ring(z, 1, 8), core), device(x, y, ring(z, -1, 8), core)
    across = device(x, y, ring(z, 4, 8), core)

    barrier = pltpu.get_barrier_semaphore()
    spot = y * 4 + x
    plane = [(spot + s) % 16 for s in range(1, 16)]
    others = [device(at % 4, at // 4, z, c) for at in plane for c in range(2)]
    others += [twin, across] + [device(x, y, ring(z, s, 8), core) for s in (1, -1, 2, -2)]
    for other in others:
        pl.semaphore_signal(barrier, inc=1, device_id=other, device_id_type=MESH)
    pack(task_ref, owner_ref, slot_ref, z, wide, packed, info)
    pl.semaphore_wait(barrier, len(others))

    sent = []

    def remote(src, dst, send, recv, to):
        return pltpu.make_async_remote_copy(
            src_ref=src, dst_ref=dst, send_sem=send, recv_sem=recv, device_id=to, device_id_type=MESH
        )

    def launch(src, dst, send, recv, to):
        copy = remote(src, dst, send, recv, to)
        copy.start()
        sent.append(copy)
        return copy

    def home(src, dst, index):
        copy = pltpu.make_async_copy(src, dst, t_local.at[index])
        copy.start()
        return copy

    def over_z(source, target, base, own):
        copies = []
        for index, (shift, low_unit, size) in enumerate(UNITS[1:]):
            units = pl.ds(low_unit, size)
            to = device(x, y, ring(z, shift, 8), core)
            at = base + index
            copies.append(launch(source.at[:, units], target.at[:, units], t_send.at[at], t_recv.at[at], to))
        return copies, home(source.at[:, pl.ds(0, 2)], target.at[:, pl.ds(0, 2)], own)

    def over_plane(source, target, recv, base, own):
        for index, at in enumerate(plane):
            to = device(at % 4, at // 4, z, core)
            launch(source(at), target.at[spot], t_send.at[base + index], t_recv.at[recv], to)
        copy = home(source(spot), target.at[spot], own)
        several = target.at[pl.ds(0, 15)]

        def arrived():
            remote(several, several, t_send.at[0], t_recv.at[recv], twin).wait_recv()
            copy.wait()

        return arrived

    def over_plane_across(source, target, recv, base):
        for index, at in enumerate([*plane, spot]):
            to = device(at % 4, at // 4, z, 1 - core)
            launch(source.at[at], target.at[spot], t_send.at[base + index], t_recv.at[recv], to)

        def arrived():
            remote(target, target, t_send.at[0], t_recv.at[recv], twin).wait_recv()

        return arrived

    info_copies = []
    for index, (shift, _, _) in enumerate(UNITS[1:]):
        to = device(x, y, ring(z, shift, 8), core)
        info_copies.append(launch(info.at[0], info_z.at[index], t_send.at[index], t_recv.at[index], to))
    z_tasks, z_home = over_z(packed.at[core], by_z, 5, 0)
    plane_b = over_plane_across(packed.at[1 - core], by_xy, 13, 13)
    for copy in info_copies:
        copy.wait_recv()
    unit = iota((8, 128), 0)
    merged = info[0]
    for index, (_, low_unit, size) in enumerate(UNITS[1:]):
        fits = jnp.logical_and(unit >= low_unit, unit < low_unit + size)
        merged = jnp.where(fits, info_z[index], merged)
    info[1] = merged
    plane_i = over_plane(lambda at: info.at[1], info_xy.at[0], 14, 29, 1)
    for copy in z_tasks:
        copy.wait_recv()
    z_home.wait()
    plane_a = over_plane(lambda at: by_z.at[at], got.at[0], 15, 44, 2)
    plane_b()
    z_more, z_more_home = over_z(by_xy, got.at[1], 9, 3)
    plane_i()
    twin_info = launch(info_xy.at[0], info_xy.at[1], t_send.at[59], t_recv.at[16], twin)
    plane_a()
    twin_info.wait_recv()
    for copy in z_more:
        copy.wait_recv()
    z_more_home.wait()
    assemble(
        got, info_xy, core * 16 + spot, row * 512, col * 1024 + layer * HALF,
        p_pattern_ref, occ_ref, wide, rows, d_ref,
    )

    y_copies = []
    for q in range(4):
        for p in range(2):
            for c in range(2):
                to_y = 2 * core + p
                mine = jnp.logical_and(to_y == y, core == c)
                src = d_ref.at[q // 2, q % 2, c, :, pl.ds(p * 256, 256)]
                dst = a.at[z, q, y, c]
                copy = remote(src, dst, y_send.at[q * 4 + p * 2 + c], y_recv.at[q, y], device(x, to_y, z, c))
                own = pltpu.make_async_copy(src, dst, local_sem.at[q])

                @pl.when(jnp.logical_not(mine))
                def _():
                    copy.start()

                @pl.when(mine)
                def _():
                    own.start()

                y_copies.append((mine, copy))

    def x_first(source, panel, sems, home_sem):
        mine = panel(x)
        up = launch(source, mine, x_send.at[sems], x_recv.at[sems], up_x)
        down = launch(source, mine, x_send.at[sems + 1], x_recv.at[sems + 1], down_x)
        home = pltpu.make_async_copy(source, mine, local_sem.at[home_sem])
        home.start()
        return up, down, home

    x_one = x_first(d_ref, lambda xx: b.at[:, xx], 0, 4)

    def x_second(pieces, sems, first):
        first[0].wait_recv()
        ref = pieces(ring(x, -1, 4), 0)
        up = launch(ref, ref, x_send.at[sems + 2], x_recv.at[sems + 2], up_x)
        first[1].wait_recv()
        ref = pieces(ring(x, 1, 4), 1)
        down = launch(ref, ref, x_send.at[sems + 3], x_recv.at[sems + 3], down_x)
        return up, down

    def y_arrived(q):
        for source_y in range(4):
            mine = jnp.logical_and(y == source_y, core == y // 2)
            block = a.at[z, q, source_y, core]

            @pl.when(jnp.logical_not(mine))
            def _():
                remote(block, block, y_send.at[0], y_recv.at[q, source_y], twin).wait_recv()

            @pl.when(mine)
            def _():
                pltpu.make_async_copy(block, block, local_sem.at[q]).wait()

    z_copies = {}

    def blocks(q, step):
        if step == 4:
            return ((ring(z, -4, 8), 0, 2), (ring(z, 4, 8), 2, 2))
        return ((ring(z, -step, 8), 0, 4), (ring(z, step, 8), 0, 4))

    def z_issue(q, step):
        (up_block, _, _), (down_block, _, _) = blocks(q, step - 1)
        size = 4 if step < 4 else 2
        index = q * 8 + (step - 1) * 2
        ref = a.at[up_block, q, pl.ds(0, size), core]
        up = launch(ref, ref, z_send.at[index], z_recv.at[index], up_z)
        ref = a.at[down_block, q, pl.ds(4 - size, size), core]
        down = launch(ref, ref, z_send.at[index + 1], z_recv.at[index + 1], down_z)
        z_copies[q, step] = (up, down)

    def twin_refs(q, step, side):
        if step == 0:
            return [(q * 9, a.at[z, q, :, side])]
        return [
            (q * 9 + step * 2 - 1 + k, a.at[block, q, pl.ds(low_y, size), side])
            for k, (block, low_y, size) in enumerate(blocks(q, step))
        ]

    def hand_over(q, step):
        for index, ref in twin_refs(q, step, core):
            launch(ref, ref, twin_send.at[index], twin_recv.at[index], twin)

    def z_arrived(q, step):
        for copy in z_copies[q, step]:
            copy.wait_recv()
        hand_over(q, step)

    def product(q, parts, first):
        def body(m, carry):
            total = None
            for zz, piece in parts:
                left = a[zz, q, pl.ds(2 * m, 2)].reshape(256, 256)
                term = dot(left, piece[...].reshape(256, 512))
                total = term if total is None else total + term
            total = total.reshape(2, 2, 64, 512)
            at = pl.ds(2 * m, 2)
            acc[q, at] = total if first else acc[q, at] + total
            return carry

        lax.fori_loop(0, 2, body, 0)

    r_copies = {}
    up_t, down_t, far_t = ring(y, 1, 4), ring(y, -1, 4), ring(y, 2, 4)

    def reduce_issue(n, k, q):
        base = (n * 4 + k) * 6

        def send(j, src, dst, to):
            r_copies[n, k, j] = launch(src, dst, r_send.at[base + j], r_recv.at[base + j], to)

        for side, to in ((0, up_y), (1, down_y)):
            far[n, k, side] = acc[q, far_t, side].astype(BF16)
            send(side, far.at[n, k, side], far_in.at[n, k, side], to)
        for side, t, to in ((0, up_t, up_y), (1, down_t, down_y)):
            near[n, k, side, 1 - side] = acc[q, t, 1 - side].astype(BF16)
            send(2 + side, near.at[n, k, side, 1 - side], near_in.at[n, k, side, 1 - side], to)

    def reduce_pass(n, k, q):
        base = (n * 4 + k) * 6
        for side, t, to in ((0, up_t, up_y), (1, down_t, down_y)):
            r_copies[n, k, side].wait_recv()
            near[n, k, side, side] = (acc[q, t, side] + far_in[n, k, side].astype(F32)).astype(BF16)
            r_copies[n, k, 4 + side] = launch(
                near.at[n, k, side, side], near_in.at[n, k, side, side],
                r_send.at[base + 4 + side], r_recv.at[base + 4 + side], to,
            )

    def reduce_end(n, k, q):
        for j in range(2, 6):
            r_copies[n, k, j].wait_recv()
        return acc[q, y] + near_in[n, k, 0].astype(F32) + near_in[n, k, 1].astype(F32)

    x_copies = {}

    def gather_issue(q):
        value = reduce_end(0, q, q)
        keep[q] = value
        low[q] = value.astype(BF16)
        x_copies[q] = x_first(low.at[q], lambda xx: b2.at[q // 2, xx, q % 2], 4 + 4 * q, 5 + q)

    def gather_pass(q):
        x_copies[q] += x_second(lambda xx, s: b2.at[q // 2, xx, q % 2, s], 4 + 4 * q, x_copies[q])

    def gather_end(q):
        x_copies[q][2].wait()
        for copy in x_copies[q][3:]:
            copy.wait_recv()

    def all_arrived(q):
        for step in range(5):
            for index, ref in twin_refs(q, step, 1 - core):
                remote(ref, ref, twin_send.at[index], twin_recv.at[index], twin).wait_recv()

    def square(q):
        all_arrived(q)
        product(q, [(zz, b.at[zz // 4, zz % 4]) for zz in range(8)], True)
        reduce_issue(0, q, q)

    for q in range(4):
        y_arrived(q)
        hand_over(q, 0)
        if q < 3:
            z_issue(q, 1)

    def pass_on(q, step, *then):
        z_arrived(q, step)
        if then:
            z_issue(*then)

    pass_on(0, 1, 0, 2)
    pass_on(1, 1, 1, 2)
    pass_on(2, 1, 3, 1)
    pass_on(0, 2, 0, 3)
    x_two = x_second(lambda xx, s: b.at[s, xx], 0, x_one)
    pass_on(1, 2, 2, 2)
    pass_on(3, 1, 1, 3)
    pass_on(0, 3, 0, 4)
    pass_on(2, 2, 3, 2)
    pass_on(1, 3, 2, 3)
    pass_on(0, 4, 1, 4)
    for copy in x_two:
        copy.wait_recv()
    x_one[2].wait()
    square(0)
    pass_on(3, 2, 3, 3)
    pass_on(2, 3, 2, 4)
    reduce_pass(0, 0, 0)
    pass_on(1, 4)
    square(1)
    pass_on(3, 3, 3, 4)
    gather_issue(0)
    reduce_pass(0, 1, 1)
    pass_on(2, 4)
    square(2)
    gather_pass(0)
    gather_issue(1)
    pass_on(3, 4)
    square(3)
    gather_pass(1)
    reduce_pass(0, 2, 2)
    reduce_pass(0, 3, 3)
    gather_end(0)
    gather_end(1)
    for q in range(2):
        product(q, [(zz, b2.at[0, zz]) for zz in range(4)], True)
    gather_issue(2)
    gather_issue(3)
    for q in range(2, 4):
        product(q, [(zz, b2.at[0, zz]) for zz in range(4)], True)
    gather_pass(2)
    gather_pass(3)
    gather_end(2)
    gather_end(3)
    order = [1 - layer, 3 - layer, layer, 2 + layer]
    swaps = []

    def start(k):
        product(order[k], [(4 + zz, b2.at[1, zz]) for zz in range(4)], False)
        reduce_issue(1, k, order[k])

    def finish(k):
        q = order[k]
        value = (3.0 * keep[q] - 2.0 * reduce_end(1, k, q)).astype(BF16)
        if k < 2:
            result[k] = value
            swaps.append(launch(result.at[k], other_ref.at[k], swap_send.at[k], swap_recv.at[k], across))
        else:
            own_ref[k - 2] = value

    start(0)
    start(1)
    reduce_pass(1, 0, order[0])
    start(2)
    reduce_pass(1, 1, order[1])
    finish(0)
    start(3)
    reduce_pass(1, 2, order[2])
    finish(1)
    reduce_pass(1, 3, order[3])
    finish(2)
    finish(3)
    for copy in swaps:
        copy.wait_recv()

    for mine, copy in y_copies:
        @pl.when(jnp.logical_not(mine))
        def _():
            copy.wait_send()

    for copy in sent:
        copy.wait_send()


def place_kernel(own_ref, other_ref, pattern_ref, out_ref):
    layer = lax.axis_index("layer")
    spread = (iota((16, 1024), 0) == iota((16, 1024), 1) // BLK).astype(F32)
    mask_all = dot(pattern_ref[...].astype(F32), spread)
    mask = jnp.where(layer == 0, mask_all[0:4], mask_all[4:8])
    source = iota((256, 256), 0)
    want = iota((256, 256), 1)
    side = jnp.where(source < 128, layer, 1 - layer)
    goes = ((source % 128) // HALF) * BLK + side * HALF + source % HALF
    place = (goes == want).astype(BF16)
    for half in range(2):
        own = own_ref[half].reshape(128, 512)
        other = other_ref[half].reshape(128, 512)
        for t in range(4):
            both = jnp.concatenate([own[:, t * 128 : (t + 1) * 128], other[:, t * 128 : (t + 1) * 128]], axis=1)
            full = dot(both, place)
            for blk in range(4):
                out_ref[blk * BLK + half * HALF : blk * BLK + (half + 1) * HALF, t * 256 : (t + 1) * 256] = (
                    full[blk * HALF : (blk + 1) * HALF] * mask[blk : blk + 1, t * 256 : (t + 1) * 256]
                )


VMEM = pl.BlockSpec(memory_space=pltpu.VMEM)


def on_device(tasks, task_owner, task_slot, p_pattern, c_pattern, occupations):
    dma = pltpu.SemaphoreType.DMA
    count = tasks.shape[0]
    own, other = pl.pallas_call(
        step_kernel,
        out_shape=[jax.ShapeDtypeStruct((2, 2, 64, 512), BF16)] * 2,
        in_specs=[VMEM] * 5,
        out_specs=[VMEM] * 2,
        scratch_shapes=[
            pltpu.VMEM((4096, 128), F32),
            pltpu.VMEM((2, 16, 8, 16, 128), BF16),
            pltpu.VMEM((16, 8, 16, 128), BF16),
            pltpu.VMEM((16, 8, 16, 128), BF16),
            pltpu.VMEM((2, 16, 8, 16, 128), BF16),
            pltpu.VMEM((2, 8, 128), F32),
            pltpu.VMEM((4, 8, 128), F32),
            pltpu.VMEM((2, 16, 8, 128), F32),
            pltpu.VMEM((512, 512), F32),
            pltpu.VMEM((2, 2, 2, 64, 512), BF16),
            dma((4,)),
            dma((60,)),
            dma((17,)),
            pltpu.VMEM((8, 4, 4, 2, 64, 256), BF16),
            pltpu.VMEM((2, 4, 2, 2, 64, 512), BF16),
            pltpu.VMEM((2, 4, 2, 2, 64, 512), BF16),
            pltpu.VMEM((4, 4, 2, 64, 512), F32),
            pltpu.VMEM((4, 2, 64, 512), F32),
            pltpu.VMEM((4, 2, 64, 512), BF16),
            pltpu.VMEM((2, 4, 2, 2, 64, 512), BF16),
            pltpu.VMEM((2, 4, 2, 64, 512), BF16),
            pltpu.VMEM((2, 4, 2, 2, 64, 512), BF16),
            pltpu.VMEM((2, 4, 2, 64, 512), BF16),
            pltpu.VMEM((2, 2, 64, 512), BF16),
            dma((9,)),
            dma((16,)),
            dma((4, 4)),
            dma((32,)),
            dma((32,)),
            dma((36,)),
            dma((36,)),
            dma((20,)),
            dma((20,)),
            dma((48,)),
            dma((48,)),
            dma((2,)),
            dma((2,)),
        ],
        compiler_params=pltpu.CompilerParams(
            vmem_limit_bytes=56 << 20, collective_id=0, has_side_effects=True
        ),
        name="purify",
    )(
        tasks, task_owner.reshape(1, count), task_slot.reshape(1, count), p_pattern,
        occupations.reshape(4, 2 * BLK),
    )
    return pl.pallas_call(
        place_kernel,
        out_shape=jax.ShapeDtypeStruct((256, 1024), F32),
        in_specs=[VMEM] * 3,
        out_specs=VMEM,
        compiler_params=pltpu.CompilerParams(vmem_limit_bytes=16 << 20),
        name="place",
    )(own, other, c_pattern)


def solution(mesh):
    return jax.shard_map(
        on_device,
        mesh=mesh,
        in_specs=(
            P(("row", "col"), None),
            P(("row", "col"), None),
            P(("row", "col")),
            P("row", "col"),
            P("row", "col"),
            P("row"),
        ),
        out_specs=P(("row", "layer"), "col"),
        check_vma=False,
    )
```

```python
import functools

import jax
import jax.numpy as jnp
from jax import lax
from jax.experimental import pallas as pl
from jax.experimental.pallas import tpu as pltpu
from jax.sharding import PartitionSpec as P

BLK = 64
HALF = 32
MESH = pl.DeviceIdType.MESH
BF16 = jnp.bfloat16
F32 = jnp.float32


def iota(shape, axis):
    return lax.broadcasted_iota(jnp.int32, shape, axis)


def dot(a, b):
    return jnp.dot(a, b, preferred_element_type=F32)


def pack(task_ref, owner_ref, slot_ref, z, core, wide, packed, info):
    count = task_ref.shape[0]
    owner = owner_ref[...]
    column = jnp.transpose(jnp.broadcast_to(owner.astype(F32), (count, count))).astype(jnp.int32)
    earlier = iota((count, count), 0) < iota((count, count), 1)
    placed = jnp.sum(jnp.logical_and(column == owner, earlier).astype(jnp.int32), axis=0, keepdims=True)
    line = iota((256, count), 0)
    group = (line // 2) % 4
    to_core = line // 128
    shift = jnp.where(group == 0, 0, jnp.where(group == 1, 1, -1))
    shift = jnp.where(group == 3, jnp.where(to_core == core, 2, -2), shift)
    there = (z + shift + 8) % 8
    wanted = (((line // 8) % 4) * 4 + (line // 32) % 4) * 8 + (there % 4) * 2 + to_core
    put = jnp.logical_and(owner == wanted, placed == line % 2)
    halves = jnp.concatenate(
        [jnp.logical_and(put, there // 4 == h).astype(F32) for h in range(2)], axis=1
    ).astype(BF16)
    lane = iota((256, 256), 0)
    goes = iota((256, 256), 1)
    source = ((goes % 128) // HALF) * BLK + (goes // 128) * HALF + goes % HALF
    pick = (lane == source).astype(BF16)
    for half in range(2):
        for quad in range(8):
            p = half * 8 + quad
            piece = dot(task_ref[:, p * 256 : (p + 1) * 256], pick).astype(BF16)
            both = jnp.concatenate([piece[:, :128], piece[:, 128:]], axis=0)
            wide[half, pl.ds(quad, 256, stride=8), :] = dot(halves, both)
        for to in range(2):
            value = wide[half, to * 1024 : (to + 1) * 1024, :].astype(BF16)
            packed[half, to] = value.reshape(16, 4, 16, 128)
    slot = slot_ref[...]
    order = (slot % 16) * 8 + slot // 16 + 1
    mark = jnp.sum(jnp.where(put, order, 0).astype(F32), axis=1, keepdims=True)
    at = iota((256, 128), 1) == iota((256, 128), 0) // 8
    rows = (iota((8, 256), 0) == iota((8, 256), 1) % 8).astype(BF16)
    info[0] = dot(rows, jnp.where(at, mark, 0.0).astype(BF16)) - 1.0


def find_slots(info, lane, marks):
    tiles = jnp.concatenate([info[k].reshape(128, 128) for k in range(2)], axis=0)
    slot = jnp.sum(jnp.where(iota((256, 128), 1) == lane, tiles, 0.0), axis=1, keepdims=True)
    marks[...] = jnp.transpose(jnp.where(slot == iota((256, 128), 1).astype(F32), 1.0, 0.0)).astype(BF16)


def assemble(half, got, marks, row_id, col_id, pattern_ref, occ_ref, wide, rows, out_ref):
    for k in range(2):
        wide[half, k * 1024 : (k + 1) * 1024, :] = got[half, k].reshape(1024, 128).astype(F32)
    spread = (iota((16, 512), 0) == iota((16, 512), 1) // HALF).astype(F32)
    mask = dot(pattern_ref[...].astype(F32), spread)
    column = col_id + (iota((8, 512), 1) // HALF) * BLK + iota((8, 512), 1) % HALF
    first = row_id + iota((8, 512), 0) * BLK
    quarter = iota((8, 128), 1) // HALF
    doubled = jnp.concatenate([occ_ref[r // 2 : r // 2 + 1, :] for r in range(8)], axis=0)
    occ = jnp.where(iota((8, 128), 0) % 2 == 0, doubled, pltpu.roll(doubled, BLK, 1))
    for quad in range(8):
        summed = dot(marks[...], wide[half, pl.ds(quad, 256, stride=8), :].astype(BF16))
        for e in range(4):
            tiles = []
            for t in range(4):
                tile = None
                for f in range(4):
                    block = t * 4 + f
                    value = summed[block * 8 : (block + 1) * 8, :]
                    shift = (f - e) % 4
                    if shift:
                        value = pltpu.roll(value, shift * HALF, 1)
                    tile = value if tile is None else jnp.where(quarter == f, value, tile)
                tiles.append(tile)
            i = quad * 4 + e
            full = half * HALF + i
            line = jnp.concatenate(tiles, axis=1) * mask
            line = line + jnp.where(first + full == column, occ[:, full : full + 1], 0.0)
            rows[half, i * 8 : (i + 1) * 8, :] = line
    want = iota((256, 256), 0)
    have = iota((256, 256), 1)
    move = (have == (want % HALF) * 8 + want // HALF).astype(BF16)
    out_ref[half] = dot(move, rows[half].astype(BF16)).astype(BF16).reshape(2, 2, 64, 512)


def step_kernel(
    task_hbm, owner_hbm, slot_hbm, p_pattern_hbm, occ_hbm, own_ref, other_ref,
    task_ref, owner_ref, slot_ref, p_pattern_ref, occ_ref, load_sem, marks,
    wide, packed, by_z, by_xy, got, info, info_z, info_xy, rows, d_ref,
    t_local, t_send, t_recv, a, b, b2, acc, keep, low, near, far, near_in, far_in, result,
    local_sem, y_send, y_recv, z_send, z_recv, twin_send, twin_recv,
    x_send, x_recv, r_send, r_recv, swap_send, swap_recv,
):
    row, col, layer = lax.axis_index("row"), lax.axis_index("col"), lax.axis_index("layer")
    x, y = row // 4, row % 4
    core = col % 2
    z = layer * 4 + col // 2

    def device(xx, yy, zz, cc):
        return (xx * 4 + yy, (zz % 4) * 2 + cc, zz // 4)

    def ring(value, step, size):
        return (value + step + size) % size

    twin = device(x, y, z, 1 - core)
    up_y, down_y = device(x, ring(y, 1, 4), z, core), device(x, ring(y, -1, 4), z, core)
    up_x, down_x = device(ring(x, 1, 4), y, z, core), device(ring(x, -1, 4), y, z, core)
    up_z, down_z = device(x, y, ring(z, 1, 8), core), device(x, y, ring(z, -1, 8), core)
    across = device(x, y, ring(z, 4, 8), core)

    barrier = pltpu.get_barrier_semaphore()
    spot = y * 4 + x
    plane = [(spot + s) % 16 for s in range(1, 16)]
    others = [device(at % 4, at // 4, z, c) for at in plane for c in range(2)]
    others += [twin, across] + [device(x, y, ring(z, s, 8), core) for s in (1, -1, 2, -2)]
    for other in others:
        pl.semaphore_signal(barrier, inc=1, device_id=other, device_id_type=MESH)
    loads = [
        pltpu.make_async_copy(src, dst, load_sem.at[index])
        for index, (src, dst) in enumerate((
            (owner_hbm, owner_ref), (slot_hbm, slot_ref), (task_hbm, task_ref),
            (p_pattern_hbm, p_pattern_ref), (occ_hbm, occ_ref),
        ))
    ]
    for load in loads:
        load.start()
    for load in loads:
        load.wait()
    pack(task_ref, owner_ref, slot_ref, z, core, wide, packed, info)
    pl.semaphore_wait(barrier, len(others))

    sent = []

    def remote(src, dst, send, recv, to):
        return pltpu.make_async_remote_copy(
            src_ref=src, dst_ref=dst, send_sem=send, recv_sem=recv, device_id=to, device_id_type=MESH
        )

    def launch(src, dst, send, recv, to):
        copy = remote(src, dst, send, recv, to)
        copy.start()
        sent.append(copy)
        return copy

    def home(src, dst, index):
        copy = pltpu.make_async_copy(src, dst, t_local.at[index])
        copy.start()
        return copy

    def over_z(source, target, far_shift, base, own):
        copies = []
        for index, shift in enumerate((1, -1, far_shift)):
            to = device(x, y, ring(z, shift, 8), core)
            at = base + index
            copies.append(
                launch(source.at[:, index + 1], target.at[:, index + 1], t_send.at[at], t_recv.at[at], to)
            )
        copy = home(source.at[:, 0], target.at[:, 0], own)

        def arrived():
            for c in copies:
                c.wait_recv()
            copy.wait()

        return arrived

    def over_plane(source, target, recv, base, own):
        for index, at in enumerate(plane):
            to = device(at % 4, at // 4, z, core)
            launch(source(at), target.at[spot], t_send.at[base + index], t_recv.at[recv], to)
        copy = home(source(spot), target.at[spot], own)
        several = target.at[pl.ds(0, 15)]

        def arrived():
            remote(several, several, t_send.at[0], t_recv.at[recv], twin).wait_recv()
            copy.wait()

        return arrived

    def over_plane_across(source, target, recv, base):
        for index, at in enumerate([*plane, spot]):
            to = device(at % 4, at // 4, z, 1 - core)
            launch(source.at[at], target.at[spot], t_send.at[base + index], t_recv.at[recv], to)

        def arrived():
            remote(target, target, t_send.at[0], t_recv.at[recv], twin).wait_recv()

        return arrived

    info_copies = []
    for index, shift in enumerate((1, -1, 2)):
        to = device(x, y, ring(z, shift, 8), core)
        info_copies.append(launch(info.at[0], info_z.at[index], t_send.at[index], t_recv.at[index], to))
    z_tasks, plane_b = [], []
    for half in range(2):
        z_tasks.append(over_z(packed.at[half, core], by_z.at[half], 2, 3 + 6 * half, half))
        plane_b.append(
            over_plane_across(packed.at[half, 1 - core], by_xy.at[half], 15 + half, 32 + 32 * half)
        )
    for copy in info_copies:
        copy.wait_recv()
    group = iota((8, 128), 0) // 2
    merged = info[0]
    for index in range(3):
        merged = jnp.where(group == index + 1, info_z[index], merged)
    info[1] = merged
    plane_i = over_plane(lambda at: info.at[1], info_xy.at[0], 17, 96, 2)
    plane_a, z_more = [], []
    for half in range(2):
        z_tasks[half]()
        plane_a.append(
            over_plane(lambda at: by_z.at[half, at], got.at[half, 0], 18 + half, 112 + 16 * half, 3 + half)
        )
        plane_b[half]()
        z_more.append(over_z(by_xy.at[half], got.at[half, 1], -2, 6 + 6 * half, 5 + half))
    plane_i()
    twin_info = launch(info_xy.at[0], info_xy.at[1], t_send.at[144], t_recv.at[20], twin)

    def tasks_arrived(half):
        plane_a[half]()
        z_more[half]()
        if half == 0:
            twin_info.wait_recv()
            find_slots(info_xy, core * 16 + spot, marks)
        assemble(
            half, got, marks, row * 512, col * 1024 + layer * HALF,
            p_pattern_ref, occ_ref, wide, rows, d_ref,
        )

    y_copies = []

    def y_issue(q):
        for p in range(2):
            for c in range(2):
                to_y = 2 * core + p
                mine = jnp.logical_and(to_y == y, core == c)
                src = d_ref.at[q // 2, q % 2, c, :, pl.ds(p * 256, 256)]
                dst = a.at[z, q, y, c]
                copy = remote(src, dst, y_send.at[q * 4 + p * 2 + c], y_recv.at[q, y], device(x, to_y, z, c))
                own = pltpu.make_async_copy(src, dst, local_sem.at[q])

                @pl.when(jnp.logical_not(mine))
                def _():
                    copy.start()

                @pl.when(mine)
                def _():
                    own.start()

                y_copies.append((mine, copy))

    def x_first(source, panel, sems, home_sem):
        mine = panel(x)
        up = launch(source, mine, x_send.at[sems], x_recv.at[sems], up_x)
        down = launch(source, mine, x_send.at[sems + 1], x_recv.at[sems + 1], down_x)
        home = pltpu.make_async_copy(source, mine, local_sem.at[home_sem])
        home.start()
        return up, down, home

    def x_second(pieces, sems, first):
        first[0].wait_recv()
        ref = pieces(ring(x, -1, 4), 0)
        up = launch(ref, ref, x_send.at[sems + 2], x_recv.at[sems + 2], up_x)
        first[1].wait_recv()
        ref = pieces(ring(x, 1, 4), 1)
        down = launch(ref, ref, x_send.at[sems + 3], x_recv.at[sems + 3], down_x)
        return up, down

    def y_arrived(q):
        for source_y in range(4):
            mine = jnp.logical_and(y == source_y, core == y // 2)
            block = a.at[z, q, source_y, core]

            @pl.when(jnp.logical_not(mine))
            def _():
                remote(block, block, y_send.at[0], y_recv.at[q, source_y], twin).wait_recv()

            @pl.when(mine)
            def _():
                pltpu.make_async_copy(block, block, local_sem.at[q]).wait()

    z_copies = {}

    def blocks(q, step):
        if step == 4:
            return ((ring(z, -4, 8), 0, 2), (ring(z, 4, 8), 2, 2))
        return ((ring(z, -step, 8), 0, 4), (ring(z, step, 8), 0, 4))

    def z_issue(q, step):
        (up_block, _, _), (down_block, _, _) = blocks(q, step - 1)
        size = 4 if step < 4 else 2
        index = q * 8 + (step - 1) * 2
        ref = a.at[up_block, q, pl.ds(0, size), core]
        up = launch(ref, ref, z_send.at[index], z_recv.at[index], up_z)
        ref = a.at[down_block, q, pl.ds(4 - size, size), core]
        down = launch(ref, ref, z_send.at[index + 1], z_recv.at[index + 1], down_z)
        z_copies[q, step] = (up, down)

    def twin_refs(q, step, side):
        if step == 0:
            return [(q * 9, a.at[z, q, :, side])]
        return [
            (q * 9 + step * 2 - 1 + k, a.at[block, q, pl.ds(low_y, size), side])
            for k, (block, low_y, size) in enumerate(blocks(q, step))
        ]

    def hand_over(q, step):
        for index, ref in twin_refs(q, step, core):
            launch(ref, ref, twin_send.at[index], twin_recv.at[index], twin)

    def z_arrived(q, step):
        for copy in z_copies[q, step]:
            copy.wait_recv()
        hand_over(q, step)

    def product(q, parts, first):
        def body(m, carry):
            total = None
            for zz, piece in parts:
                left = a[zz, q, pl.ds(2 * m, 2)].reshape(256, 256)
                term = dot(left, piece[...].reshape(256, 512))
                total = term if total is None else total + term
            total = total.reshape(2, 2, 64, 512)
            at = pl.ds(2 * m, 2)
            acc[q, at] = total if first else acc[q, at] + total
            return carry

        lax.fori_loop(0, 2, body, 0)

    r_copies = {}
    up_t, down_t, far_t = ring(y, 1, 4), ring(y, -1, 4), ring(y, 2, 4)

    def reduce_issue(n, k, q):
        base = (n * 4 + k) * 6

        def send(j, src, dst, to):
            r_copies[n, k, j] = launch(src, dst, r_send.at[base + j], r_recv.at[base + j], to)

        for side, to in ((0, up_y), (1, down_y)):
            far[n, k, side] = acc[q, far_t, side].astype(BF16)
            send(side, far.at[n, k, side], far_in.at[n, k, side], to)
        for side, t, to in ((0, up_t, up_y), (1, down_t, down_y)):
            near[n, k, side, 1 - side] = acc[q, t, 1 - side].astype(BF16)
            send(2 + side, near.at[n, k, side, 1 - side], near_in.at[n, k, side, 1 - side], to)

    def reduce_pass(n, k, q):
        base = (n * 4 + k) * 6
        for side, t, to in ((0, up_t, up_y), (1, down_t, down_y)):
            r_copies[n, k, side].wait_recv()
            near[n, k, side, side] = (acc[q, t, side] + far_in[n, k, side].astype(F32)).astype(BF16)
            r_copies[n, k, 4 + side] = launch(
                near.at[n, k, side, side], near_in.at[n, k, side, side],
                r_send.at[base + 4 + side], r_recv.at[base + 4 + side], to,
            )

    def reduce_end(n, k, q):
        for j in range(2, 6):
            r_copies[n, k, j].wait_recv()
        return acc[q, y] + near_in[n, k, 0].astype(F32) + near_in[n, k, 1].astype(F32)

    x_copies = {}

    def gather_issue(q):
        value = reduce_end(0, q, q)
        keep[q] = value
        low[q] = value.astype(BF16)
        x_copies[q] = x_first(low.at[q], lambda xx: b2.at[q // 2, xx, q % 2], 4 + 4 * q, 5 + q)

    def gather_pass(q):
        x_copies[q] += x_second(lambda xx, s: b2.at[q // 2, xx, q % 2, s], 4 + 4 * q, x_copies[q])

    def gather_end(q):
        x_copies[q][2].wait()
        for copy in x_copies[q][3:]:
            copy.wait_recv()

    def all_arrived(q):
        for step in range(5):
            for index, ref in twin_refs(q, step, 1 - core):
                remote(ref, ref, twin_send.at[index], twin_recv.at[index], twin).wait_recv()

    def square(q):
        all_arrived(q)
        product(q, [(zz, b.at[zz // 4, zz % 4]) for zz in range(8)], True)
        reduce_issue(0, q, q)

    tasks_arrived(0)
    y_issue(0)
    y_issue(1)
    b_rows = [x_first(d_ref.at[0], lambda xx: b.at[0, xx], 20, 4)]
    tasks_arrived(1)
    y_issue(2)
    y_issue(3)
    b_rows.append(x_first(d_ref.at[1], lambda xx: b.at[1, xx], 22, 9))
    for q in range(4):
        y_arrived(q)
        hand_over(q, 0)
        if q < 3:
            z_issue(q, 1)

    def pass_on(q, step, *then):
        z_arrived(q, step)
        if then:
            z_issue(*then)

    pass_on(0, 1, 0, 2)
    pass_on(1, 1, 1, 2)
    pass_on(2, 1, 3, 1)
    pass_on(0, 2, 0, 3)
    b_rows[0][0].wait_recv()
    below = b.at[0, ring(x, -1, 4)]
    b_far = [launch(below, below, x_send.at[0], x_recv.at[0], up_x)]
    b_rows[1][1].wait_recv()
    above = b.at[1, ring(x, 1, 4)]
    b_far.append(launch(above, above, x_send.at[1], x_recv.at[1], down_x))
    pass_on(1, 2, 2, 2)
    pass_on(3, 1, 1, 3)
    pass_on(0, 3, 0, 4)
    pass_on(2, 2, 3, 2)
    pass_on(1, 3, 2, 3)
    pass_on(0, 4, 1, 4)
    for copy in (b_rows[0][1], b_rows[1][0], *b_far):
        copy.wait_recv()
    for copies in b_rows:
        copies[2].wait()
    square(0)
    pass_on(3, 2, 3, 3)
    pass_on(2, 3, 2, 4)
    reduce_pass(0, 0, 0)
    pass_on(1, 4)
    square(1)
    pass_on(3, 3, 3, 4)
    gather_issue(0)
    reduce_pass(0, 1, 1)
    pass_on(2, 4)
    square(2)
    gather_pass(0)
    gather_issue(1)
    pass_on(3, 4)
    square(3)
    gather_pass(1)
    reduce_pass(0, 2, 2)
    reduce_pass(0, 3, 3)
    gather_end(0)
    gather_end(1)
    for q in range(2):
        product(q, [(zz, b2.at[0, zz]) for zz in range(4)], True)
    gather_issue(2)
    gather_issue(3)
    for q in range(2, 4):
        product(q, [(zz, b2.at[0, zz]) for zz in range(4)], True)
    gather_pass(2)
    gather_pass(3)
    gather_end(2)
    gather_end(3)
    order = [1 - layer, 3 - layer, layer, 2 + layer]
    swaps = []

    def start(k):
        product(order[k], [(4 + zz, b2.at[1, zz]) for zz in range(4)], False)
        reduce_issue(1, k, order[k])

    def finish(k):
        q = order[k]
        value = (3.0 * keep[q] - 2.0 * reduce_end(1, k, q)).astype(BF16)
        if k < 2:
            result[k] = value
            swaps.append(launch(result.at[k], other_ref.at[k], swap_send.at[k], swap_recv.at[k], across))
        else:
            own_ref[k - 2] = value

    start(0)
    start(1)
    reduce_pass(1, 0, order[0])
    start(2)
    reduce_pass(1, 1, order[1])
    finish(0)
    start(3)
    reduce_pass(1, 2, order[2])
    finish(1)
    reduce_pass(1, 3, order[3])
    finish(2)
    finish(3)
    for copy in swaps:
        copy.wait_recv()

    for mine, copy in y_copies:
        @pl.when(jnp.logical_not(mine))
        def _():
            copy.wait_send()

    for copy in sent:
        copy.wait_send()


def place_kernel(own_ref, other_ref, pattern_ref, out_ref):
    layer = lax.axis_index("layer")
    spread = (iota((16, 1024), 0) == iota((16, 1024), 1) // BLK).astype(F32)
    mask_all = dot(pattern_ref[...].astype(F32), spread)
    mask = jnp.where(layer == 0, mask_all[0:4], mask_all[4:8])
    source = iota((256, 256), 0)
    want = iota((256, 256), 1)
    side = jnp.where(source < 128, layer, 1 - layer)
    goes = ((source % 128) // HALF) * BLK + side * HALF + source % HALF
    place = (goes == want).astype(BF16)
    for half in range(2):
        own = own_ref[half].reshape(128, 512)
        other = other_ref[half].reshape(128, 512)
        for t in range(4):
            both = jnp.concatenate([own[:, t * 128 : (t + 1) * 128], other[:, t * 128 : (t + 1) * 128]], axis=1)
            full = dot(both, place)
            for blk in range(4):
                out_ref[blk * BLK + half * HALF : blk * BLK + (half + 1) * HALF, t * 256 : (t + 1) * 256] = (
                    full[blk * HALF : (blk + 1) * HALF] * mask[blk : blk + 1, t * 256 : (t + 1) * 256]
                )


VMEM = pl.BlockSpec(memory_space=pltpu.VMEM)


def on_device(tasks, task_owner, task_slot, p_pattern, c_pattern, occupations):
    dma = pltpu.SemaphoreType.DMA
    count = tasks.shape[0]
    own, other = pl.pallas_call(
        step_kernel,
        out_shape=[jax.ShapeDtypeStruct((2, 2, 64, 512), BF16)] * 2,
        in_specs=[pl.BlockSpec(memory_space=pl.ANY)] * 5,
        out_specs=[VMEM] * 2,
        scratch_shapes=[
            pltpu.VMEM(tasks.shape, BF16),
            pltpu.VMEM((1, count), jnp.int32),
            pltpu.VMEM((1, count), jnp.int32),
            pltpu.VMEM(p_pattern.shape, jnp.int32),
            pltpu.VMEM((4, 2 * BLK), F32),
            dma((5,)),
            pltpu.VMEM((128, 256), BF16),
            pltpu.VMEM((2, 2048, 128), F32),
            pltpu.VMEM((2, 2, 16, 4, 16, 128), BF16),
            pltpu.VMEM((2, 16, 4, 16, 128), BF16),
            pltpu.VMEM((2, 16, 4, 16, 128), BF16),
            pltpu.VMEM((2, 2, 16, 4, 16, 128), BF16),
            pltpu.VMEM((2, 8, 128), F32),
            pltpu.VMEM((3, 8, 128), F32),
            pltpu.VMEM((2, 16, 8, 128), F32),
            pltpu.VMEM((2, 256, 512), F32),
            pltpu.VMEM((2, 2, 2, 64, 512), BF16),
            dma((7,)),
            dma((145,)),
            dma((21,)),
            pltpu.VMEM((8, 4, 4, 2, 64, 256), BF16),
            pltpu.VMEM((2, 4, 2, 2, 64, 512), BF16),
            pltpu.VMEM((2, 4, 2, 2, 64, 512), BF16),
            pltpu.VMEM((4, 4, 2, 64, 512), F32),
            pltpu.VMEM((4, 2, 64, 512), F32),
            pltpu.VMEM((4, 2, 64, 512), BF16),
            pltpu.VMEM((2, 4, 2, 2, 64, 512), BF16),
            pltpu.VMEM((2, 4, 2, 64, 512), BF16),
            pltpu.VMEM((2, 4, 2, 2, 64, 512), BF16),
            pltpu.VMEM((2, 4, 2, 64, 512), BF16),
            pltpu.VMEM((2, 2, 64, 512), BF16),
            dma((10,)),
            dma((16,)),
            dma((4, 4)),
            dma((32,)),
            dma((32,)),
            dma((36,)),
            dma((36,)),
            dma((24,)),
            dma((24,)),
            dma((48,)),
            dma((48,)),
            dma((2,)),
            dma((2,)),
        ],
        compiler_params=pltpu.CompilerParams(
            vmem_limit_bytes=56 << 20, collective_id=0, has_side_effects=True
        ),
        name="purify",
    )(
        tasks, task_owner.reshape(1, count), task_slot.reshape(1, count), p_pattern,
        occupations.reshape(4, 2 * BLK),
    )
    return pl.pallas_call(
        place_kernel,
        out_shape=jax.ShapeDtypeStruct((256, 1024), F32),
        in_specs=[VMEM] * 3,
        out_specs=VMEM,
        compiler_params=pltpu.CompilerParams(vmem_limit_bytes=16 << 20),
        name="place",
    )(own, other, c_pattern)


def solution(mesh):
    return jax.shard_map(
        on_device,
        mesh=mesh,
        in_specs=(
            P(("row", "col"), None),
            P(("row", "col"), None),
            P(("row", "col")),
            P("row", "col"),
            P("row", "col"),
            P("row"),
        ),
        out_specs=P(("row", "layer"), "col"),
        check_vma=False,
    )
```

```python
import functools

import jax
import jax.numpy as jnp
from jax import lax
from jax.experimental import pallas as pl
from jax.experimental.pallas import tpu as pltpu
from jax.sharding import PartitionSpec as P

BLK = 64
HALF = 32
MESH = pl.DeviceIdType.MESH
BF16 = jnp.bfloat16
F32 = jnp.float32


def iota(shape, axis):
    return lax.broadcasted_iota(jnp.int32, shape, axis)


def dot(a, b):
    return jnp.dot(a, b, preferred_element_type=F32)


def pack(task_ref, owner_ref, slot_ref, z, core, wide, packed, info):
    count = task_ref.shape[0]
    owner = owner_ref[...]
    column = jnp.transpose(jnp.broadcast_to(owner.astype(F32), (count, count))).astype(jnp.int32)
    earlier = iota((count, count), 0) < iota((count, count), 1)
    placed = jnp.sum(jnp.logical_and(column == owner, earlier).astype(jnp.int32), axis=0, keepdims=True)
    line = iota((256, count), 0)
    group = (line // 2) % 4
    to_core = line // 128
    shift = jnp.where(group == 0, 0, jnp.where(group == 1, 1, -1))
    shift = jnp.where(group == 3, jnp.where(to_core == core, 2, -2), shift)
    there = (z + shift + 8) % 8
    wanted = (((line // 8) % 4) * 4 + (line // 32) % 4) * 8 + (there % 4) * 2 + to_core
    put = jnp.logical_and(owner == wanted, placed == line % 2)
    halves = jnp.concatenate(
        [jnp.logical_and(put, there // 4 == h).astype(F32) for h in range(2)], axis=1
    ).astype(BF16)
    lane = iota((256, 256), 0)
    goes = iota((256, 256), 1)
    source = ((goes % 128) // HALF) * BLK + (goes // 128) * HALF + goes % HALF
    pick = (lane == source).astype(BF16)
    for half in range(2):
        for quad in range(8):
            p = half * 8 + quad
            piece = dot(task_ref[:, p * 256 : (p + 1) * 256], pick).astype(BF16)
            both = jnp.concatenate([piece[:, :128], piece[:, 128:]], axis=0)
            wide[half, pl.ds(quad, 256, stride=8), :] = dot(halves, both)
        for to in range(2):
            value = wide[half, to * 1024 : (to + 1) * 1024, :].astype(BF16)
            packed[half, to] = value.reshape(16, 4, 16, 128)
    slot = slot_ref[...]
    order = (slot % 16) * 8 + slot // 16 + 1
    mark = jnp.sum(jnp.where(put, order, 0).astype(F32), axis=1, keepdims=True)
    at = iota((256, 128), 1) == iota((256, 128), 0) // 8
    rows = (iota((8, 256), 0) == iota((8, 256), 1) % 8).astype(BF16)
    info[0] = dot(rows, jnp.where(at, mark, 0.0).astype(BF16)) - 1.0


def find_slots(info, lane, marks):
    tiles = jnp.concatenate([info[k].reshape(128, 128) for k in range(2)], axis=0)
    slot = jnp.sum(jnp.where(iota((256, 128), 1) == lane, tiles, 0.0), axis=1, keepdims=True)
    marks[...] = jnp.transpose(jnp.where(slot == iota((256, 128), 1).astype(F32), 1.0, 0.0)).astype(BF16)


def assemble(half, got, marks, row_id, col_id, pattern_ref, occ_ref, wide, rows, out_ref):
    for k in range(2):
        wide[half, k * 1024 : (k + 1) * 1024, :] = got[half, k].reshape(1024, 128).astype(F32)
    spread = (iota((16, 512), 0) == iota((16, 512), 1) // HALF).astype(F32)
    mask = dot(pattern_ref[...].astype(F32), spread)
    column = col_id + (iota((8, 512), 1) // HALF) * BLK + iota((8, 512), 1) % HALF
    first = row_id + iota((8, 512), 0) * BLK
    quarter = iota((8, 128), 1) // HALF
    doubled = jnp.concatenate([occ_ref[r // 2 : r // 2 + 1, :] for r in range(8)], axis=0)
    occ = jnp.where(iota((8, 128), 0) % 2 == 0, doubled, pltpu.roll(doubled, BLK, 1))
    for quad in range(8):
        summed = dot(marks[...], wide[half, pl.ds(quad, 256, stride=8), :].astype(BF16))
        for e in range(4):
            tiles = []
            for t in range(4):
                tile = None
                for f in range(4):
                    block = t * 4 + f
                    value = summed[block * 8 : (block + 1) * 8, :]
                    shift = (f - e) % 4
                    if shift:
                        value = pltpu.roll(value, shift * HALF, 1)
                    tile = value if tile is None else jnp.where(quarter == f, value, tile)
                tiles.append(tile)
            i = quad * 4 + e
            full = half * HALF + i
            line = jnp.concatenate(tiles, axis=1) * mask
            line = line + jnp.where(first + full == column, occ[:, full : full + 1], 0.0)
            rows[half, i * 8 : (i + 1) * 8, :] = line
    want = iota((256, 256), 0)
    have = iota((256, 256), 1)
    move = (have == (want % HALF) * 8 + want // HALF).astype(BF16)
    out_ref[half] = dot(move, rows[half].astype(BF16)).astype(BF16).reshape(2, 2, 64, 512)


def step_kernel(
    task_hbm, owner_hbm, slot_hbm, p_pattern_hbm, occ_hbm, own_ref, other_ref,
    task_ref, owner_ref, slot_ref, p_pattern_ref, occ_ref, load_sem, marks,
    wide, packed, by_z, by_xy, got, info, info_z, info_xy, rows, d_ref,
    t_local, t_send, t_recv, a, b, b2, acc, keep, low, near, far, near_in, far_in, result,
    local_sem, y_send, y_recv, z_send, z_recv, twin_send, twin_recv,
    x_send, x_recv, r_send, r_recv, swap_send, swap_recv,
):
    row, col, layer = lax.axis_index("row"), lax.axis_index("col"), lax.axis_index("layer")
    x, y = row // 4, row % 4
    core = col % 2
    z = layer * 4 + col // 2

    def device(xx, yy, zz, cc):
        return (xx * 4 + yy, (zz % 4) * 2 + cc, zz // 4)

    def ring(value, step, size):
        return (value + step + size) % size

    twin = device(x, y, z, 1 - core)
    up_y, down_y = device(x, ring(y, 1, 4), z, core), device(x, ring(y, -1, 4), z, core)
    up_x, down_x = device(ring(x, 1, 4), y, z, core), device(ring(x, -1, 4), y, z, core)
    up_z, down_z = device(x, y, ring(z, 1, 8), core), device(x, y, ring(z, -1, 8), core)
    across = device(x, y, ring(z, 4, 8), core)

    barrier = pltpu.get_barrier_semaphore()
    spot = y * 4 + x
    plane = [(spot + s) % 16 for s in range(1, 16)]
    others = [device(at % 4, at // 4, z, c) for at in plane for c in range(2)]
    others += [twin, across] + [device(x, y, ring(z, s, 8), core) for s in (1, -1, 2, -2)]
    for other in others:
        pl.semaphore_signal(barrier, inc=1, device_id=other, device_id_type=MESH)
    loads = [
        pltpu.make_async_copy(src, dst, load_sem.at[index])
        for index, (src, dst) in enumerate((
            (owner_hbm, owner_ref), (slot_hbm, slot_ref), (task_hbm, task_ref),
            (p_pattern_hbm, p_pattern_ref), (occ_hbm, occ_ref),
        ))
    ]
    for load in loads:
        load.start()
    for load in loads:
        load.wait()
    pack(task_ref, owner_ref, slot_ref, z, core, wide, packed, info)
    pl.semaphore_wait(barrier, len(others))

    sent = []

    def remote(src, dst, send, recv, to):
        return pltpu.make_async_remote_copy(
            src_ref=src, dst_ref=dst, send_sem=send, recv_sem=recv, device_id=to, device_id_type=MESH
        )

    def launch(src, dst, send, recv, to):
        copy = remote(src, dst, send, recv, to)
        copy.start()
        sent.append(copy)
        return copy

    def home(src, dst, index):
        copy = pltpu.make_async_copy(src, dst, t_local.at[index])
        copy.start()
        return copy

    def over_z(source, target, far_shift, base, own):
        copies = []
        for index, shift in enumerate((1, -1, far_shift)):
            to = device(x, y, ring(z, shift, 8), core)
            at = base + index
            copies.append(
                launch(source.at[:, index + 1], target.at[:, index + 1], t_send.at[at], t_recv.at[at], to)
            )
        copy = home(source.at[:, 0], target.at[:, 0], own)

        def arrived():
            for c in copies:
                c.wait_recv()
            copy.wait()

        return arrived

    def over_plane(source, target, recv, base, own):
        for index, at in enumerate(plane):
            to = device(at % 4, at // 4, z, core)
            launch(source(at), target.at[spot], t_send.at[base + index], t_recv.at[recv], to)
        copy = home(source(spot), target.at[spot], own)
        several = target.at[pl.ds(0, 15)]

        def arrived():
            remote(several, several, t_send.at[0], t_recv.at[recv], twin).wait_recv()
            copy.wait()

        return arrived

    def over_plane_across(source, target, recv, base):
        for index, at in enumerate([*plane, spot]):
            to = device(at % 4, at // 4, z, 1 - core)
            launch(source.at[at], target.at[spot], t_send.at[base + index], t_recv.at[recv], to)

        def arrived():
            remote(target, target, t_send.at[0], t_recv.at[recv], twin).wait_recv()

        return arrived

    info_copies = []
    for index, shift in enumerate((1, -1, 2)):
        to = device(x, y, ring(z, shift, 8), core)
        info_copies.append(launch(info.at[0], info_z.at[index], t_send.at[index], t_recv.at[index], to))
    z_tasks, plane_b = [], []
    for half in range(2):
        z_tasks.append(over_z(packed.at[half, core], by_z.at[half], 2, 3 + 6 * half, half))
        plane_b.append(
            over_plane_across(packed.at[half, 1 - core], by_xy.at[half], 15 + half, 32 + 32 * half)
        )
    for copy in info_copies:
        copy.wait_recv()
    group = iota((8, 128), 0) // 2
    merged = info[0]
    for index in range(3):
        merged = jnp.where(group == index + 1, info_z[index], merged)
    info[1] = merged
    plane_i = over_plane(lambda at: info.at[1], info_xy.at[0], 17, 96, 2)
    plane_a, z_more = [], []
    for half in range(2):
        z_tasks[half]()
        plane_a.append(
            over_plane(lambda at: by_z.at[half, at], got.at[half, 0], 18 + half, 112 + 16 * half, 3 + half)
        )
        plane_b[half]()
        z_more.append(over_z(by_xy.at[half], got.at[half, 1], -2, 6 + 6 * half, 5 + half))
    plane_i()
    twin_info = launch(info_xy.at[0], info_xy.at[1], t_send.at[144], t_recv.at[20], twin)

    def tasks_arrived(half):
        plane_a[half]()
        z_more[half]()
        if half == 0:
            twin_info.wait_recv()
            find_slots(info_xy, core * 16 + spot, marks)
        assemble(
            half, got, marks, row * 512, col * 1024 + layer * HALF,
            p_pattern_ref, occ_ref, wide, rows, d_ref,
        )

    y_copies = []

    def y_issue(q):
        for p in range(2):
            for c in range(2):
                to_y = 2 * core + p
                mine = jnp.logical_and(to_y == y, core == c)
                src = d_ref.at[q // 2, q % 2, c, :, pl.ds(p * 256, 256)]
                dst = a.at[z, q, y, c]
                copy = remote(src, dst, y_send.at[q * 4 + p * 2 + c], y_recv.at[q, y], device(x, to_y, z, c))
                own = pltpu.make_async_copy(src, dst, local_sem.at[q])

                @pl.when(jnp.logical_not(mine))
                def _():
                    copy.start()

                @pl.when(mine)
                def _():
                    own.start()

                y_copies.append((mine, copy))

    def x_first(source, panel, sems, home_sem):
        mine = panel(x)
        up = launch(source, mine, x_send.at[sems], x_recv.at[sems], up_x)
        down = launch(source, mine, x_send.at[sems + 1], x_recv.at[sems + 1], down_x)
        home = pltpu.make_async_copy(source, mine, local_sem.at[home_sem])
        home.start()
        return up, down, home

    def y_arrived(q):
        for source_y in range(4):
            mine = jnp.logical_and(y == source_y, core == y // 2)
            block = a.at[z, q, source_y, core]

            @pl.when(jnp.logical_not(mine))
            def _():
                remote(block, block, y_send.at[0], y_recv.at[q, source_y], twin).wait_recv()

            @pl.when(mine)
            def _():
                pltpu.make_async_copy(block, block, local_sem.at[q]).wait()

    z_copies = {}

    def blocks(q, step):
        if step == 4:
            return ((ring(z, -4, 8), 0, 2), (ring(z, 4, 8), 2, 2))
        return ((ring(z, -step, 8), 0, 4), (ring(z, step, 8), 0, 4))

    def z_issue(q, step):
        (up_block, _, _), (down_block, _, _) = blocks(q, step - 1)
        size = 4 if step < 4 else 2
        index = q * 8 + (step - 1) * 2
        ref = a.at[up_block, q, pl.ds(0, size), core]
        up = launch(ref, ref, z_send.at[index], z_recv.at[index], up_z)
        ref = a.at[down_block, q, pl.ds(4 - size, size), core]
        down = launch(ref, ref, z_send.at[index + 1], z_recv.at[index + 1], down_z)
        z_copies[q, step] = (up, down)

    def twin_refs(q, step, side):
        if step == 0:
            return [(q * 9, a.at[z, q, :, side])]
        return [
            (q * 9 + step * 2 - 1 + k, a.at[block, q, pl.ds(low_y, size), side])
            for k, (block, low_y, size) in enumerate(blocks(q, step))
        ]

    def hand_over(q, step):
        for index, ref in twin_refs(q, step, core):
            launch(ref, ref, twin_send.at[index], twin_recv.at[index], twin)

    def z_arrived(q, step):
        for copy in z_copies[q, step]:
            copy.wait_recv()
        hand_over(q, step)

    def product(q, parts, first):
        def body(m, carry):
            total = None
            for zz, piece in parts:
                left = a[zz, q, pl.ds(2 * m, 2)].reshape(256, 256)
                term = dot(left, piece[...].reshape(256, 512))
                total = term if total is None else total + term
            total = total.reshape(2, 2, 64, 512)
            at = pl.ds(2 * m, 2)
            acc[q, at] = total if first else acc[q, at] + total
            return carry

        lax.fori_loop(0, 2, body, 0)

    r_copies = {}
    up_t, down_t, far_t = ring(y, 1, 4), ring(y, -1, 4), ring(y, 2, 4)

    def reduce_issue(n, k, q):
        base = (n * 4 + k) * 6

        def send(j, src, dst, to):
            r_copies[n, k, j] = launch(src, dst, r_send.at[base + j], r_recv.at[base + j], to)

        for side, to in ((0, up_y), (1, down_y)):
            far[n, k, side] = acc[q, far_t, side].astype(BF16)
            send(side, far.at[n, k, side], far_in.at[n, k, side], to)
        for side, t, to in ((0, up_t, up_y), (1, down_t, down_y)):
            near[n, k, side, 1 - side] = acc[q, t, 1 - side].astype(BF16)
            send(2 + side, near.at[n, k, side, 1 - side], near_in.at[n, k, side, 1 - side], to)

    def reduce_pass(n, k, q):
        base = (n * 4 + k) * 6
        for side, t, to in ((0, up_t, up_y), (1, down_t, down_y)):
            r_copies[n, k, side].wait_recv()
            near[n, k, side, side] = (acc[q, t, side] + far_in[n, k, side].astype(F32)).astype(BF16)
            r_copies[n, k, 4 + side] = launch(
                near.at[n, k, side, side], near_in.at[n, k, side, side],
                r_send.at[base + 4 + side], r_recv.at[base + 4 + side], to,
            )

    def reduce_end(n, k, q):
        for j in range(2, 6):
            r_copies[n, k, j].wait_recv()
        return acc[q, y] + near_in[n, k, 0].astype(F32) + near_in[n, k, 1].astype(F32)

    x_copies = {}

    def gather_issue(q):
        value = reduce_end(0, q, q)
        keep[q] = value
        low[q] = value.astype(BF16)
        sems = 4 + 6 * q
        here = pltpu.make_async_copy(low.at[q], b2.at[q // 2, x, q % 2], local_sem.at[5 + q])
        here.start()
        copies = [None] * 4
        for part in range(2):
            for side, to in ((0, up_x), (1, down_x)):
                half = part if side == 0 else 1 - part
                at = sems + 2 * part + side
                copies[2 * part + side] = launch(
                    low.at[q, half], b2.at[q // 2, x, q % 2, half], x_send.at[at], x_recv.at[at], to
                )
        x_copies[q] = (here, copies)

    def gather_pass(q):
        copies = x_copies[q][1]
        for side, to, source in ((0, up_x, ring(x, -1, 4)), (1, down_x, ring(x, 1, 4))):
            copies[side].wait_recv()
            ref = b2.at[q // 2, source, q % 2, side]
            at = 4 + 6 * q + 4 + side
            copies.append(launch(ref, ref, x_send.at[at], x_recv.at[at], to))

    def gather_end(q):
        here, copies = x_copies[q]
        here.wait()
        for copy in copies[2:]:
            copy.wait_recv()

    def all_arrived(q):
        for step in range(5):
            for index, ref in twin_refs(q, step, 1 - core):
                remote(ref, ref, twin_send.at[index], twin_recv.at[index], twin).wait_recv()

    def square(q):
        all_arrived(q)
        product(q, [(zz, b.at[zz // 4, zz % 4]) for zz in range(8)], True)
        reduce_issue(0, q, q)

    tasks_arrived(0)
    y_issue(0)
    y_issue(1)
    b_rows = [x_first(d_ref.at[0], lambda xx: b.at[0, xx], 28, 4)]
    tasks_arrived(1)
    y_issue(2)
    y_issue(3)
    b_rows.append(x_first(d_ref.at[1], lambda xx: b.at[1, xx], 30, 9))
    for q in range(4):
        y_arrived(q)
        hand_over(q, 0)
        if q < 3:
            z_issue(q, 1)

    def pass_on(q, step, *then):
        z_arrived(q, step)
        if then:
            z_issue(*then)

    pass_on(0, 1, 0, 2)
    pass_on(1, 1, 1, 2)
    pass_on(2, 1, 3, 1)
    pass_on(0, 2, 0, 3)
    b_rows[0][0].wait_recv()
    below = b.at[0, ring(x, -1, 4)]
    b_far = [launch(below, below, x_send.at[0], x_recv.at[0], up_x)]
    b_rows[1][1].wait_recv()
    above = b.at[1, ring(x, 1, 4)]
    b_far.append(launch(above, above, x_send.at[1], x_recv.at[1], down_x))
    pass_on(1, 2, 2, 2)
    pass_on(3, 1, 1, 3)
    pass_on(0, 3, 0, 4)
    pass_on(2, 2, 3, 2)
    pass_on(1, 3, 2, 3)
    pass_on(0, 4, 1, 4)
    for copy in (b_rows[0][1], b_rows[1][0], *b_far):
        copy.wait_recv()
    for copies in b_rows:
        copies[2].wait()
    square(0)
    pass_on(3, 2, 3, 3)
    pass_on(2, 3, 2, 4)
    reduce_pass(0, 0, 0)
    pass_on(1, 4)
    square(1)
    pass_on(3, 3, 3, 4)
    gather_issue(0)
    reduce_pass(0, 1, 1)
    pass_on(2, 4)
    square(2)
    gather_pass(0)
    gather_issue(1)
    pass_on(3, 4)
    square(3)
    gather_pass(1)
    reduce_pass(0, 2, 2)
    reduce_pass(0, 3, 3)
    gather_end(0)
    gather_end(1)
    for q in range(2):
        product(q, [(zz, b2.at[0, zz]) for zz in range(4)], True)
    gather_issue(2)
    gather_issue(3)
    for q in range(2, 4):
        product(q, [(zz, b2.at[0, zz]) for zz in range(4)], True)
    gather_pass(2)
    gather_pass(3)
    gather_end(2)
    gather_end(3)
    order = [1 - layer, 3 - layer, layer, 2 + layer]
    swaps = []

    def start(k):
        product(order[k], [(4 + zz, b2.at[1, zz]) for zz in range(4)], False)
        reduce_issue(1, k, order[k])

    def finish(k):
        q = order[k]
        value = (3.0 * keep[q] - 2.0 * reduce_end(1, k, q)).astype(BF16)
        if k < 2:
            result[k] = value
            swaps.append(launch(result.at[k], other_ref.at[k], swap_send.at[k], swap_recv.at[k], across))
        else:
            own_ref[k - 2] = value

    start(0)
    start(1)
    reduce_pass(1, 0, order[0])
    start(2)
    reduce_pass(1, 1, order[1])
    finish(0)
    start(3)
    reduce_pass(1, 2, order[2])
    finish(1)
    reduce_pass(1, 3, order[3])
    finish(2)
    finish(3)
    for copy in swaps:
        copy.wait_recv()

    for mine, copy in y_copies:
        @pl.when(jnp.logical_not(mine))
        def _():
            copy.wait_send()

    for copy in sent:
        copy.wait_send()


def place_kernel(own_hbm, other_hbm, pattern_hbm, out_hbm, own_ref, other_ref, pattern_ref, out_ref, load_sem, store_sem):
    layer = lax.axis_index("layer")
    loads = [
        pltpu.make_async_copy(src, dst, load_sem.at[index])
        for index, (src, dst) in enumerate(
            ((pattern_hbm, pattern_ref), (own_hbm, own_ref), (other_hbm, other_ref))
        )
    ]
    for load in loads:
        load.start()
    for load in loads:
        load.wait()
    spread = (iota((16, 1024), 0) == iota((16, 1024), 1) // BLK).astype(F32)
    mask_all = dot(pattern_ref[...].astype(F32), spread)
    mask = jnp.where(layer == 0, mask_all[0:4], mask_all[4:8])
    source = iota((256, 256), 0)
    want = iota((256, 256), 1)
    side = jnp.where(source < 128, layer, 1 - layer)
    goes = ((source % 128) // HALF) * BLK + side * HALF + source % HALF
    place = (goes == want).astype(BF16)
    stores = []
    for t in range(4):
        for half in range(2):
            own = own_ref[half].reshape(128, 512)
            other = other_ref[half].reshape(128, 512)
            both = jnp.concatenate([own[:, t * 128 : (t + 1) * 128], other[:, t * 128 : (t + 1) * 128]], axis=1)
            full = dot(both, place)
            for blk in range(4):
                out_ref[blk * BLK + half * HALF : blk * BLK + (half + 1) * HALF, t * 256 : (t + 1) * 256] = (
                    full[blk * HALF : (blk + 1) * HALF] * mask[blk : blk + 1, t * 256 : (t + 1) * 256]
                )
        span = pl.ds(t * 256, 256)
        store = pltpu.make_async_copy(out_ref.at[:, span], out_hbm.at[:, span], store_sem.at[t])
        store.start()
        stores.append(store)
    for store in stores:
        store.wait()


VMEM = pl.BlockSpec(memory_space=pltpu.VMEM)


def on_device(tasks, task_owner, task_slot, p_pattern, c_pattern, occupations):
    dma = pltpu.SemaphoreType.DMA
    count = tasks.shape[0]
    own, other = pl.pallas_call(
        step_kernel,
        out_shape=[jax.ShapeDtypeStruct((2, 2, 64, 512), BF16)] * 2,
        in_specs=[pl.BlockSpec(memory_space=pl.ANY)] * 5,
        out_specs=[VMEM] * 2,
        scratch_shapes=[
            pltpu.VMEM(tasks.shape, BF16),
            pltpu.VMEM((1, count), jnp.int32),
            pltpu.VMEM((1, count), jnp.int32),
            pltpu.VMEM(p_pattern.shape, jnp.int32),
            pltpu.VMEM((4, 2 * BLK), F32),
            dma((5,)),
            pltpu.VMEM((128, 256), BF16),
            pltpu.VMEM((2, 2048, 128), F32),
            pltpu.VMEM((2, 2, 16, 4, 16, 128), BF16),
            pltpu.VMEM((2, 16, 4, 16, 128), BF16),
            pltpu.VMEM((2, 16, 4, 16, 128), BF16),
            pltpu.VMEM((2, 2, 16, 4, 16, 128), BF16),
            pltpu.VMEM((2, 8, 128), F32),
            pltpu.VMEM((3, 8, 128), F32),
            pltpu.VMEM((2, 16, 8, 128), F32),
            pltpu.VMEM((2, 256, 512), F32),
            pltpu.VMEM((2, 2, 2, 64, 512), BF16),
            dma((7,)),
            dma((145,)),
            dma((21,)),
            pltpu.VMEM((8, 4, 4, 2, 64, 256), BF16),
            pltpu.VMEM((2, 4, 2, 2, 64, 512), BF16),
            pltpu.VMEM((2, 4, 2, 2, 64, 512), BF16),
            pltpu.VMEM((4, 4, 2, 64, 512), F32),
            pltpu.VMEM((4, 2, 64, 512), F32),
            pltpu.VMEM((4, 2, 64, 512), BF16),
            pltpu.VMEM((2, 4, 2, 2, 64, 512), BF16),
            pltpu.VMEM((2, 4, 2, 64, 512), BF16),
            pltpu.VMEM((2, 4, 2, 2, 64, 512), BF16),
            pltpu.VMEM((2, 4, 2, 64, 512), BF16),
            pltpu.VMEM((2, 2, 64, 512), BF16),
            dma((10,)),
            dma((16,)),
            dma((4, 4)),
            dma((32,)),
            dma((32,)),
            dma((36,)),
            dma((36,)),
            dma((32,)),
            dma((32,)),
            dma((48,)),
            dma((48,)),
            dma((2,)),
            dma((2,)),
        ],
        compiler_params=pltpu.CompilerParams(
            vmem_limit_bytes=56 << 20, collective_id=0, has_side_effects=True
        ),
        name="purify",
    )(
        tasks, task_owner.reshape(1, count), task_slot.reshape(1, count), p_pattern,
        occupations.reshape(4, 2 * BLK),
    )
    return pl.pallas_call(
        place_kernel,
        out_shape=jax.ShapeDtypeStruct((256, 1024), F32),
        in_specs=[pl.BlockSpec(memory_space=pl.ANY)] * 3,
        out_specs=pl.BlockSpec(memory_space=pl.ANY),
        scratch_shapes=[
            pltpu.VMEM((2, 2, 64, 512), BF16),
            pltpu.VMEM((2, 2, 64, 512), BF16),
            pltpu.VMEM(c_pattern.shape, jnp.int32),
            pltpu.VMEM((256, 1024), F32),
            dma((3,)),
            dma((4,)),
        ],
        compiler_params=pltpu.CompilerParams(vmem_limit_bytes=56 << 20),
        name="place",
    )(own, other, c_pattern)


def solution(mesh):
    return jax.shard_map(
        on_device,
        mesh=mesh,
        in_specs=(
            P(("row", "col"), None),
            P(("row", "col"), None),
            P(("row", "col")),
            P("row", "col"),
            P("row", "col"),
            P("row"),
        ),
        out_specs=P(("row", "layer"), "col"),
        check_vma=False,
    )
```

```python
import functools

import jax
import jax.numpy as jnp
from jax import lax
from jax.experimental import pallas as pl
from jax.experimental.pallas import tpu as pltpu
from jax.sharding import PartitionSpec as P

BLK = 64
HALF = 32
MESH = pl.DeviceIdType.MESH
BF16 = jnp.bfloat16
F32 = jnp.float32


def iota(shape, axis):
    return lax.broadcasted_iota(jnp.int32, shape, axis)


def dot(a, b):
    return jnp.dot(a, b, preferred_element_type=F32)


def pack(task_ref, owner_ref, slot_ref, z, core, wide, packed, info):
    count = task_ref.shape[0]
    owner = owner_ref[...]
    column = jnp.transpose(jnp.broadcast_to(owner.astype(F32), (count, count))).astype(jnp.int32)
    earlier = iota((count, count), 0) < iota((count, count), 1)
    placed = jnp.sum(jnp.logical_and(column == owner, earlier).astype(jnp.int32), axis=0, keepdims=True)
    line = iota((256, count), 0)
    group = (line // 2) % 4
    to_core = line // 128
    shift = jnp.where(group == 0, 0, jnp.where(group == 1, 1, -1))
    shift = jnp.where(group == 3, jnp.where(to_core == core, 2, -2), shift)
    there = (z + shift + 8) % 8
    wanted = (((line // 8) % 4) * 4 + (line // 32) % 4) * 8 + (there % 4) * 2 + to_core
    put = jnp.logical_and(owner == wanted, placed == line % 2)
    halves = jnp.concatenate(
        [jnp.logical_and(put, there // 4 == h).astype(F32) for h in range(2)], axis=1
    ).astype(BF16)
    lane = iota((256, 256), 0)
    goes = iota((256, 256), 1)
    source = ((goes % 128) // HALF) * BLK + (goes // 128) * HALF + goes % HALF
    pick = (lane == source).astype(BF16)
    for half in range(2):
        for quad in range(8):
            p = half * 8 + quad
            piece = dot(task_ref[:, p * 256 : (p + 1) * 256], pick).astype(BF16)
            both = jnp.concatenate([piece[:, :128], piece[:, 128:]], axis=0)
            wide[half, pl.ds(quad, 256, stride=8), :] = dot(halves, both)
        for to in range(2):
            value = wide[half, to * 1024 : (to + 1) * 1024, :].astype(BF16)
            packed[half, to] = value.reshape(16, 4, 16, 128)
    slot = slot_ref[...]
    order = (slot % 16) * 8 + slot // 16 + 1
    mark = jnp.sum(jnp.where(put, order, 0).astype(F32), axis=1, keepdims=True)
    at = iota((256, 128), 1) == iota((256, 128), 0) // 8
    rows = (iota((8, 256), 0) == iota((8, 256), 1) % 8).astype(BF16)
    info[0] = dot(rows, jnp.where(at, mark, 0.0).astype(BF16)) - 1.0


def find_slots(info, lane, marks):
    tiles = jnp.concatenate([info[k].reshape(128, 128) for k in range(2)], axis=0)
    slot = jnp.sum(jnp.where(iota((256, 128), 1) == lane, tiles, 0.0), axis=1, keepdims=True)
    marks[...] = jnp.transpose(jnp.where(slot == iota((256, 128), 1).astype(F32), 1.0, 0.0)).astype(BF16)


def assemble(half, got, marks, row_id, col_id, pattern_ref, occ_ref, wide, rows, out_ref):
    for k in range(2):
        wide[half, k * 1024 : (k + 1) * 1024, :] = got[half, k].reshape(1024, 128).astype(F32)
    spread = (iota((16, 512), 0) == iota((16, 512), 1) // HALF).astype(F32)
    mask = dot(pattern_ref[...].astype(F32), spread)
    column = col_id + (iota((8, 512), 1) // HALF) * BLK + iota((8, 512), 1) % HALF
    first = row_id + iota((8, 512), 0) * BLK
    quarter = iota((8, 128), 1) // HALF
    doubled = jnp.concatenate([occ_ref[r // 2 : r // 2 + 1, :] for r in range(8)], axis=0)
    occ = jnp.where(iota((8, 128), 0) % 2 == 0, doubled, pltpu.roll(doubled, BLK, 1))
    for quad in range(8):
        summed = dot(marks[...], wide[half, pl.ds(quad, 256, stride=8), :].astype(BF16))
        for e in range(4):
            tiles = []
            for t in range(4):
                tile = None
                for f in range(4):
                    block = t * 4 + f
                    value = summed[block * 8 : (block + 1) * 8, :]
                    shift = (f - e) % 4
                    if shift:
                        value = pltpu.roll(value, shift * HALF, 1)
                    tile = value if tile is None else jnp.where(quarter == f, value, tile)
                tiles.append(tile)
            i = quad * 4 + e
            full = half * HALF + i
            line = jnp.concatenate(tiles, axis=1) * mask
            line = line + jnp.where(first + full == column, occ[:, full : full + 1], 0.0)
            rows[half, i * 8 : (i + 1) * 8, :] = line
    want = iota((256, 256), 0)
    have = iota((256, 256), 1)
    move = (have == (want % HALF) * 8 + want // HALF).astype(BF16)
    out_ref[half] = dot(move, rows[half].astype(BF16)).astype(BF16).reshape(2, 2, 64, 512)


def step_kernel(
    task_hbm, owner_hbm, slot_hbm, p_pattern_hbm, occ_hbm, own_ref, other_ref,
    task_ref, owner_ref, slot_ref, p_pattern_ref, occ_ref, load_sem, marks,
    wide, packed, by_z, by_xy, got, info, info_z, info_xy, rows, d_ref,
    t_local, t_send, t_recv, a, b, b2, acc, keep, low, near, far, near_in, far_in, result,
    local_sem, y_send, y_recv, z_send, z_recv, twin_send, twin_recv,
    x_send, x_recv, r_send, r_recv, swap_send, swap_recv,
):
    row, col, layer = lax.axis_index("row"), lax.axis_index("col"), lax.axis_index("layer")
    x, y = row // 4, row % 4
    core = col % 2
    z = layer * 4 + col // 2

    def device(xx, yy, zz, cc):
        return (xx * 4 + yy, (zz % 4) * 2 + cc, zz // 4)

    def ring(value, step, size):
        return (value + step + size) % size

    twin = device(x, y, z, 1 - core)
    up_y, down_y = device(x, ring(y, 1, 4), z, core), device(x, ring(y, -1, 4), z, core)
    up_x, down_x = device(ring(x, 1, 4), y, z, core), device(ring(x, -1, 4), y, z, core)
    up_z, down_z = device(x, y, ring(z, 1, 8), core), device(x, y, ring(z, -1, 8), core)
    across = device(x, y, ring(z, 4, 8), core)

    barrier = pltpu.get_barrier_semaphore()
    spot = y * 4 + x
    plane = [(spot + s) % 16 for s in range(1, 16)]
    others = [device(at % 4, at // 4, z, c) for at in plane for c in range(2)]
    others += [twin, across] + [device(x, y, ring(z, s, 8), core) for s in (1, -1, 2, -2)]
    for other in others:
        pl.semaphore_signal(barrier, inc=1, device_id=other, device_id_type=MESH)
    loads = [
        pltpu.make_async_copy(src, dst, load_sem.at[index])
        for index, (src, dst) in enumerate((
            (owner_hbm, owner_ref), (slot_hbm, slot_ref), (task_hbm, task_ref),
            (p_pattern_hbm, p_pattern_ref), (occ_hbm, occ_ref),
        ))
    ]
    for load in loads:
        load.start()
    for load in loads:
        load.wait()
    pack(task_ref, owner_ref, slot_ref, z, core, wide, packed, info)
    pl.semaphore_wait(barrier, len(others))

    sent = []

    def remote(src, dst, send, recv, to):
        return pltpu.make_async_remote_copy(
            src_ref=src, dst_ref=dst, send_sem=send, recv_sem=recv, device_id=to, device_id_type=MESH
        )

    def launch(src, dst, send, recv, to):
        copy = remote(src, dst, send, recv, to)
        copy.start()
        sent.append(copy)
        return copy

    def home(src, dst, index):
        copy = pltpu.make_async_copy(src, dst, t_local.at[index])
        copy.start()
        return copy

    def over_z(source, target, far_shift, base, own):
        copies = []
        for index, shift in enumerate((1, -1, far_shift)):
            to = device(x, y, ring(z, shift, 8), core)
            at = base + index
            copies.append(
                launch(source.at[:, index + 1], target.at[:, index + 1], t_send.at[at], t_recv.at[at], to)
            )
        copy = home(source.at[:, 0], target.at[:, 0], own)

        def arrived():
            for c in copies:
                c.wait_recv()
            copy.wait()

        return arrived

    def over_plane(source, target, recv, base, own):
        for index, at in enumerate(plane):
            to = device(at % 4, at // 4, z, core)
            launch(source(at), target.at[spot], t_send.at[base + index], t_recv.at[recv], to)
        copy = home(source(spot), target.at[spot], own)
        several = target.at[pl.ds(0, 15)]

        def arrived():
            remote(several, several, t_send.at[0], t_recv.at[recv], twin).wait_recv()
            copy.wait()

        return arrived

    def over_plane_across(source, target, recv, base):
        for index, at in enumerate([*plane, spot]):
            to = device(at % 4, at // 4, z, 1 - core)
            launch(source.at[at], target.at[spot], t_send.at[base + index], t_recv.at[recv], to)

        def arrived():
            remote(target, target, t_send.at[0], t_recv.at[recv], twin).wait_recv()

        return arrived

    info_copies = []
    for index, shift in enumerate((1, -1, 2)):
        to = device(x, y, ring(z, shift, 8), core)
        info_copies.append(launch(info.at[0], info_z.at[index], t_send.at[index], t_recv.at[index], to))
    z_tasks, plane_b = [], []
    for half in range(2):
        z_tasks.append(over_z(packed.at[half, core], by_z.at[half], 2, 3 + 6 * half, half))
        plane_b.append(
            over_plane_across(packed.at[half, 1 - core], by_xy.at[half], 15 + half, 32 + 32 * half)
        )
    for copy in info_copies:
        copy.wait_recv()
    group = iota((8, 128), 0) // 2
    merged = info[0]
    for index in range(3):
        merged = jnp.where(group == index + 1, info_z[index], merged)
    info[1] = merged
    plane_i = over_plane(lambda at: info.at[1], info_xy.at[0], 17, 96, 2)
    plane_a, z_more = [], []
    for half in range(2):
        z_tasks[half]()
        plane_a.append(
            over_plane(lambda at: by_z.at[half, at], got.at[half, 0], 18 + half, 112 + 16 * half, 3 + half)
        )
        plane_b[half]()
        z_more.append(over_z(by_xy.at[half], got.at[half, 1], -2, 6 + 6 * half, 5 + half))
    plane_i()
    twin_info = launch(info_xy.at[0], info_xy.at[1], t_send.at[144], t_recv.at[20], twin)

    def tasks_arrived(half):
        plane_a[half]()
        z_more[half]()
        if half == 0:
            twin_info.wait_recv()
            find_slots(info_xy, core * 16 + spot, marks)
        assemble(
            half, got, marks, row * 512, col * 1024 + layer * HALF,
            p_pattern_ref, occ_ref, wide, rows, d_ref,
        )

    y_copies = []

    def y_issue(q):
        for p in range(2):
            for c in range(2):
                to_y = 2 * core + p
                mine = jnp.logical_and(to_y == y, core == c)
                src = d_ref.at[q // 2, q % 2, c, :, pl.ds(p * 256, 256)]
                dst = a.at[z, q, y, c]
                copy = remote(src, dst, y_send.at[q * 4 + p * 2 + c], y_recv.at[q, y], device(x, to_y, z, c))
                own = pltpu.make_async_copy(src, dst, local_sem.at[q])

                @pl.when(jnp.logical_not(mine))
                def _():
                    copy.start()

                @pl.when(mine)
                def _():
                    own.start()

                y_copies.append((mine, copy))

    def x_first(source, panel, sems, home_sem):
        mine = panel(x)
        up = launch(source, mine, x_send.at[sems], x_recv.at[sems], up_x)
        down = launch(source, mine, x_send.at[sems + 1], x_recv.at[sems + 1], down_x)
        home = pltpu.make_async_copy(source, mine, local_sem.at[home_sem])
        home.start()
        return up, down, home

    def y_arrived(q):
        for source_y in range(4):
            mine = jnp.logical_and(y == source_y, core == y // 2)
            block = a.at[z, q, source_y, core]

            @pl.when(jnp.logical_not(mine))
            def _():
                remote(block, block, y_send.at[0], y_recv.at[q, source_y], twin).wait_recv()

            @pl.when(mine)
            def _():
                pltpu.make_async_copy(block, block, local_sem.at[q]).wait()

    z_copies = {}

    def blocks(q, step):
        if step == 4:
            return ((ring(z, -4, 8), 0, 2), (ring(z, 4, 8), 2, 2))
        return ((ring(z, -step, 8), 0, 4), (ring(z, step, 8), 0, 4))

    def z_issue(q, step):
        (up_block, _, _), (down_block, _, _) = blocks(q, step - 1)
        size = 4 if step < 4 else 2
        index = q * 8 + (step - 1) * 2
        ref = a.at[up_block, q, pl.ds(0, size), core]
        up = launch(ref, ref, z_send.at[index], z_recv.at[index], up_z)
        ref = a.at[down_block, q, pl.ds(4 - size, size), core]
        down = launch(ref, ref, z_send.at[index + 1], z_recv.at[index + 1], down_z)
        z_copies[q, step] = (up, down)

    def twin_refs(q, step, side):
        if step == 0:
            return [(q * 9, a.at[z, q, :, side])]
        return [
            (q * 9 + step * 2 - 1 + k, a.at[block, q, pl.ds(low_y, size), side])
            for k, (block, low_y, size) in enumerate(blocks(q, step))
        ]

    def hand_over(q, step):
        for index, ref in twin_refs(q, step, core):
            launch(ref, ref, twin_send.at[index], twin_recv.at[index], twin)

    def z_arrived(q, step):
        for copy in z_copies[q, step]:
            copy.wait_recv()
        hand_over(q, step)

    def product(q, parts, first):
        def body(m, carry):
            total = None
            for zz, piece in parts:
                left = a[zz, q, pl.ds(2 * m, 2)].reshape(256, 256)
                term = dot(left, piece[...].reshape(256, 512))
                total = term if total is None else total + term
            total = total.reshape(2, 2, 64, 512)
            at = pl.ds(2 * m, 2)
            acc[q, at] = total if first else acc[q, at] + total
            return carry

        lax.fori_loop(0, 2, body, 0)

    r_copies = {}
    up_t, down_t, far_t = ring(y, 1, 4), ring(y, -1, 4), ring(y, 2, 4)

    def reduce_issue(n, k, q):
        base = (n * 4 + k) * 6

        def send(j, src, dst, to):
            r_copies[n, k, j] = launch(src, dst, r_send.at[base + j], r_recv.at[base + j], to)

        for side, to in ((0, up_y), (1, down_y)):
            far[n, k, side] = acc[q, far_t, side].astype(BF16)
            send(side, far.at[n, k, side], far_in.at[n, k, side], to)
        for side, t, to in ((0, up_t, up_y), (1, down_t, down_y)):
            near[n, k, side, 1 - side] = acc[q, t, 1 - side].astype(BF16)
            send(2 + side, near.at[n, k, side, 1 - side], near_in.at[n, k, side, 1 - side], to)

    def reduce_pass(n, k, q):
        base = (n * 4 + k) * 6
        for side, t, to in ((0, up_t, up_y), (1, down_t, down_y)):
            r_copies[n, k, side].wait_recv()
            near[n, k, side, side] = (acc[q, t, side] + far_in[n, k, side].astype(F32)).astype(BF16)
            r_copies[n, k, 4 + side] = launch(
                near.at[n, k, side, side], near_in.at[n, k, side, side],
                r_send.at[base + 4 + side], r_recv.at[base + 4 + side], to,
            )

    def reduce_end(n, k, q):
        for j in range(2, 6):
            r_copies[n, k, j].wait_recv()
        return acc[q, y] + near_in[n, k, 0].astype(F32) + near_in[n, k, 1].astype(F32)

    x_copies = {}

    def gather_issue(q):
        value = reduce_end(0, q, q)
        keep[q] = value
        low[q] = value.astype(BF16)
        sems = 4 + 6 * q
        here = pltpu.make_async_copy(low.at[q], b2.at[q // 2, x, q % 2], local_sem.at[5 + q])
        here.start()
        copies = [None] * 4
        for part in range(2):
            for side, to in ((0, up_x), (1, down_x)):
                half = part if side == 0 else 1 - part
                at = sems + 2 * part + side
                copies[2 * part + side] = launch(
                    low.at[q, half], b2.at[q // 2, x, q % 2, half], x_send.at[at], x_recv.at[at], to
                )
        x_copies[q] = (here, copies)

    def gather_pass(q):
        copies = x_copies[q][1]
        for side, to, source in ((0, up_x, ring(x, -1, 4)), (1, down_x, ring(x, 1, 4))):
            copies[side].wait_recv()
            ref = b2.at[q // 2, source, q % 2, side]
            at = 4 + 6 * q + 4 + side
            copies.append(launch(ref, ref, x_send.at[at], x_recv.at[at], to))

    def gather_end(q):
        here, copies = x_copies[q]
        here.wait()
        for copy in copies[2:]:
            copy.wait_recv()

    def all_arrived(q):
        for step in range(5):
            for index, ref in twin_refs(q, step, 1 - core):
                remote(ref, ref, twin_send.at[index], twin_recv.at[index], twin).wait_recv()

    def square(q):
        all_arrived(q)
        product(q, [(zz, b.at[zz // 4, zz % 4]) for zz in range(8)], True)
        reduce_issue(0, q, q)

    tasks_arrived(0)
    y_issue(0)
    y_issue(1)
    b_rows = [x_first(d_ref.at[0], lambda xx: b.at[0, xx], 28, 4)]
    tasks_arrived(1)
    y_issue(2)
    y_issue(3)
    b_rows.append(x_first(d_ref.at[1], lambda xx: b.at[1, xx], 30, 9))
    for q in range(4):
        y_arrived(q)
        hand_over(q, 0)
        if q < 3:
            z_issue(q, 1)

    def pass_on(q, step, *then):
        z_arrived(q, step)
        if then:
            z_issue(*then)

    pass_on(0, 1, 0, 2)
    pass_on(1, 1, 1, 2)
    pass_on(2, 1, 3, 1)
    pass_on(0, 2, 0, 3)
    b_rows[0][0].wait_recv()
    below = b.at[0, ring(x, -1, 4)]
    b_far = [launch(below, below, x_send.at[0], x_recv.at[0], up_x)]
    b_rows[1][1].wait_recv()
    above = b.at[1, ring(x, 1, 4)]
    b_far.append(launch(above, above, x_send.at[1], x_recv.at[1], down_x))
    pass_on(1, 2, 2, 2)
    pass_on(3, 1, 1, 3)
    pass_on(0, 3, 0, 4)
    pass_on(2, 2, 3, 2)
    pass_on(1, 3, 2, 3)
    pass_on(0, 4, 1, 4)
    for copy in (b_rows[0][1], b_rows[1][0], *b_far):
        copy.wait_recv()
    for copies in b_rows:
        copies[2].wait()
    square(0)
    pass_on(3, 2, 3, 3)
    pass_on(2, 3, 2, 4)
    reduce_pass(0, 0, 0)
    pass_on(1, 4)
    square(1)
    pass_on(3, 3, 3, 4)
    gather_issue(0)
    reduce_pass(0, 1, 1)
    pass_on(2, 4)
    square(2)
    gather_pass(0)
    gather_issue(1)
    pass_on(3, 4)
    square(3)
    gather_pass(1)
    reduce_pass(0, 2, 2)
    reduce_pass(0, 3, 3)
    gather_end(0)
    gather_end(1)
    for q in range(2):
        product(q, [(zz, b2.at[0, zz]) for zz in range(4)], True)
    gather_issue(2)
    gather_issue(3)
    for q in range(2, 4):
        product(q, [(zz, b2.at[0, zz]) for zz in range(4)], True)
    gather_pass(2)
    gather_pass(3)
    gather_end(2)
    gather_end(3)
    order = [1 - layer, 3 - layer, layer, 2 + layer]
    swaps = []

    def start(k):
        product(order[k], [(4 + zz, b2.at[1, zz]) for zz in range(4)], False)
        reduce_issue(1, k, order[k])

    def finish(k):
        q = order[k]
        value = (3.0 * keep[q] - 2.0 * reduce_end(1, k, q)).astype(BF16)
        if k < 2:
            result[k] = value
            swaps.append(launch(result.at[k], other_ref.at[k], swap_send.at[k], swap_recv.at[k], across))
        else:
            own_ref[k - 2] = value

    start(0)
    start(1)
    reduce_pass(1, 0, order[0])
    start(2)
    reduce_pass(1, 1, order[1])
    start(3)
    finish(0)
    reduce_pass(1, 2, order[2])
    finish(1)
    reduce_pass(1, 3, order[3])
    finish(2)
    finish(3)
    for copy in swaps:
        copy.wait_recv()

    for mine, copy in y_copies:
        @pl.when(jnp.logical_not(mine))
        def _():
            copy.wait_send()

    for copy in sent:
        copy.wait_send()


def place_kernel(own_hbm, other_hbm, pattern_hbm, out_hbm, own_ref, other_ref, pattern_ref, out_ref, load_sem, store_sem):
    layer = lax.axis_index("layer")
    loads = [
        pltpu.make_async_copy(src, dst, load_sem.at[index])
        for index, (src, dst) in enumerate(
            ((pattern_hbm, pattern_ref), (own_hbm, own_ref), (other_hbm, other_ref))
        )
    ]
    for load in loads:
        load.start()
    for load in loads:
        load.wait()
    spread = (iota((16, 1024), 0) == iota((16, 1024), 1) // BLK).astype(F32)
    mask_all = dot(pattern_ref[...].astype(F32), spread)
    mask = jnp.where(layer == 0, mask_all[0:4], mask_all[4:8])
    source = iota((256, 256), 0)
    want = iota((256, 256), 1)
    side = jnp.where(source < 128, layer, 1 - layer)
    goes = ((source % 128) // HALF) * BLK + side * HALF + source % HALF
    place = (goes == want).astype(BF16)
    stores = []
    for t in range(4):
        for half in range(2):
            own = own_ref[half].reshape(128, 512)
            other = other_ref[half].reshape(128, 512)
            both = jnp.concatenate([own[:, t * 128 : (t + 1) * 128], other[:, t * 128 : (t + 1) * 128]], axis=1)
            full = dot(both, place)
            for blk in range(4):
                out_ref[blk * BLK + half * HALF : blk * BLK + (half + 1) * HALF, t * 256 : (t + 1) * 256] = (
                    full[blk * HALF : (blk + 1) * HALF] * mask[blk : blk + 1, t * 256 : (t + 1) * 256]
                )
        span = pl.ds(t * 256, 256)
        store = pltpu.make_async_copy(out_ref.at[:, span], out_hbm.at[:, span], store_sem.at[t])
        store.start()
        stores.append(store)
    for store in stores:
        store.wait()


VMEM = pl.BlockSpec(memory_space=pltpu.VMEM)


def on_device(tasks, task_owner, task_slot, p_pattern, c_pattern, occupations):
    dma = pltpu.SemaphoreType.DMA
    count = tasks.shape[0]
    own, other = pl.pallas_call(
        step_kernel,
        out_shape=[jax.ShapeDtypeStruct((2, 2, 64, 512), BF16)] * 2,
        in_specs=[pl.BlockSpec(memory_space=pl.ANY)] * 5,
        out_specs=[VMEM] * 2,
        scratch_shapes=[
            pltpu.VMEM(tasks.shape, BF16),
            pltpu.VMEM((1, count), jnp.int32),
            pltpu.VMEM((1, count), jnp.int32),
            pltpu.VMEM(p_pattern.shape, jnp.int32),
            pltpu.VMEM((4, 2 * BLK), F32),
            dma((5,)),
            pltpu.VMEM((128, 256), BF16),
            pltpu.VMEM((2, 2048, 128), F32),
            pltpu.VMEM((2, 2, 16, 4, 16, 128), BF16),
            pltpu.VMEM((2, 16, 4, 16, 128), BF16),
            pltpu.VMEM((2, 16, 4, 16, 128), BF16),
            pltpu.VMEM((2, 2, 16, 4, 16, 128), BF16),
            pltpu.VMEM((2, 8, 128), F32),
            pltpu.VMEM((3, 8, 128), F32),
            pltpu.VMEM((2, 16, 8, 128), F32),
            pltpu.VMEM((2, 256, 512), F32),
            pltpu.VMEM((2, 2, 2, 64, 512), BF16),
            dma((7,)),
            dma((145,)),
            dma((21,)),
            pltpu.VMEM((8, 4, 4, 2, 64, 256), BF16),
            pltpu.VMEM((2, 4, 2, 2, 64, 512), BF16),
            pltpu.VMEM((2, 4, 2, 2, 64, 512), BF16),
            pltpu.VMEM((4, 4, 2, 64, 512), F32),
            pltpu.VMEM((4, 2, 64, 512), F32),
            pltpu.VMEM((4, 2, 64, 512), BF16),
            pltpu.VMEM((2, 4, 2, 2, 64, 512), BF16),
            pltpu.VMEM((2, 4, 2, 64, 512), BF16),
            pltpu.VMEM((2, 4, 2, 2, 64, 512), BF16),
            pltpu.VMEM((2, 4, 2, 64, 512), BF16),
            pltpu.VMEM((2, 2, 64, 512), BF16),
            dma((10,)),
            dma((16,)),
            dma((4, 4)),
            dma((32,)),
            dma((32,)),
            dma((36,)),
            dma((36,)),
            dma((32,)),
            dma((32,)),
            dma((48,)),
            dma((48,)),
            dma((2,)),
            dma((2,)),
        ],
        compiler_params=pltpu.CompilerParams(
            vmem_limit_bytes=56 << 20, collective_id=0, has_side_effects=True
        ),
        name="purify",
    )(
        tasks, task_owner.reshape(1, count), task_slot.reshape(1, count), p_pattern,
        occupations.reshape(4, 2 * BLK),
    )
    return pl.pallas_call(
        place_kernel,
        out_shape=jax.ShapeDtypeStruct((256, 1024), F32),
        in_specs=[pl.BlockSpec(memory_space=pl.ANY)] * 3,
        out_specs=pl.BlockSpec(memory_space=pl.ANY),
        scratch_shapes=[
            pltpu.VMEM((2, 2, 64, 512), BF16),
            pltpu.VMEM((2, 2, 64, 512), BF16),
            pltpu.VMEM(c_pattern.shape, jnp.int32),
            pltpu.VMEM((256, 1024), F32),
            dma((3,)),
            dma((4,)),
        ],
        compiler_params=pltpu.CompilerParams(vmem_limit_bytes=56 << 20),
        name="place",
    )(own, other, c_pattern)


def solution(mesh):
    return jax.shard_map(
        on_device,
        mesh=mesh,
        in_specs=(
            P(("row", "col"), None),
            P(("row", "col"), None),
            P(("row", "col")),
            P("row", "col"),
            P("row", "col"),
            P("row"),
        ),
        out_specs=P(("row", "layer"), "col"),
        check_vma=False,
    )
```
